128 devices in a mesh: rows: 2 (over core), cols: 64 (over z, y, x).
Axes of the slice: x: 4, y: 4, z: 4, core: 2. Of those that a mesh axis runs over, the one named last changes fastest.
Arguments:
- wind_speed: float32 [16, 8192], P('rows', 'cols'), may hold values from 3 to 25
- wind_dir: float32 [16, 8192], P('rows', 'cols'), may hold values from -3.140625 to 3.140625
- depth_class: int32 [16, 8192], P('rows', 'cols'), may hold values from 0 to 3
- group_speed: float32 [4, 24], replicated, may hold values from 0.3 to 3
- dissipation: float32 [4, 24], replicated, may hold values from 0.02 to 1
- input_rate: float32 [24], replicated, may hold values from 0.02 to 0.2
- outer_spectra: float32 [131072, 864], P(('rows', 'cols')), may hold values from -6 to 6
- dest_cell: int32 [131072], P(('rows', 'cols')), may hold values from 0 to 131071, as said below
- refraction_inverse: float32 [4, 216, 216], replicated, as said below
- sweep_order: int32 [2, 4], replicated, may hold values from 0 to 3, as said below
Outputs:
- wave_action: float32 [864, 16, 8192], P(None, 'rows', 'cols')
The draws below stay inside these ranges and needn't reach their ends.
Inputs may be any that keep to these rules, and one draw needn't show every extreme that they name: `dest_cell`: every boundary point feeds a cell on the grid's outermost rows or columns. Among the points held by one device, at most 16 feed cells held by any one device, and in every draw one device receives exactly 16 points from every device. `refraction_inverse`: each matrix has a diagonal between 0.75 and 1 and off-diagonal entries below 1.2 / 216 in magnitude. `sweep_order`: each row names each of the four quadrants once.
All inputs are finite; a program needn't handle non-finite values.
Results may differ from the reference program's by a relative error of at most 0.0003.
Values sent between devices are 32-bit elements; how exact they have to be, the bound alone decides.
A program may use at most 192 MiB of HBM per device.

```python
import math
import jax
import jax.numpy as jnp
import numpy as np
from jax import lax

NDIR = 36
NFREQ = 24
NCLASS = 4
CAP = 16
ITERS = 2
R_DEV = 8
C_DEV = 128
NX = 16
NY = 8192
K = 864
KQ = 216
Q_DEV = 1024
NPTS = 131072


def draw_dest_cell(key, part):
    row_count = NX // R_DEV
    col_count = NY // C_DEV
    devices = row_count * col_count
    edge_list = [(r_id, c_id) for r_id in range(row_count) for c_id in range(col_count) if r_id == 0 or r_id == row_count - 1 or c_id == 0 or (c_id == col_count - 1)]
    edge_total = len(edge_list)
    edge_row = jnp.array(np.array([item[0] for item in edge_list], np.int32))
    edge_col = jnp.array(np.array([item[1] for item in edge_list], np.int32))
    fixed_row = jnp.array(np.array([0 if item[0] == 0 else R_DEV - 1 if item[0] == row_count - 1 else -1 for item in edge_list], np.int32))
    fixed_col = jnp.array(np.array([-1 if item[0] == 0 or item[0] == row_count - 1 else 0 if item[1] == 0 else C_DEV - 1 for item in edge_list], np.int32))
    forced = jax.random.randint(jax.random.fold_in(key, 1), (), 0, edge_total)

    def one_device(source_key):
        key_pick, key_row, key_col, key_order = jax.random.split(source_key, 4)
        others = jax.random.permutation(key_pick, (edge_total - 1) * CAP)[:Q_DEV - CAP]
        picked = others // CAP
        picked = jnp.where(picked >= forced, picked + 1, picked)
        owner_id = jnp.concatenate([jnp.full((CAP,), forced, jnp.int32), picked.astype(jnp.int32)])
        random_row = jax.random.randint(key_row, (Q_DEV,), 0, R_DEV)
        random_col = jax.random.randint(key_col, (Q_DEV,), 0, C_DEV)
        row_pick = jnp.where(fixed_row[owner_id] >= 0, fixed_row[owner_id], random_row)
        col_pick = jnp.where(fixed_col[owner_id] >= 0, fixed_col[owner_id], random_col)
        cell_id = (edge_row[owner_id] * R_DEV + row_pick) * NY + edge_col[owner_id] * C_DEV + col_pick
        shuffle = jax.random.permutation(key_order, Q_DEV)
        return cell_id[shuffle]
    device_keys = jax.random.split(jax.random.fold_in(key, 2), devices)
    return jax.vmap(one_device)(device_keys).reshape(-1).astype(jnp.int32)


def draw_refraction_inverse(key, part):
    key_diag, key_off = jax.random.split(key, 2)
    diag_vals = jax.random.uniform(key_diag, (4, KQ), jnp.float32, 0.75, 1.0)
    off_diag = jax.random.uniform(key_off, (4, KQ, KQ), jnp.float32, -1.0, 1.0) * (0.8 / KQ)
    identity = jnp.eye(KQ, dtype=jnp.float32)
    return off_diag * (1.0 - identity) + identity * diag_vals[:, :, None]


def draw_sweep_order(key, part):
    order_rows = [jax.random.permutation(jax.random.fold_in(key, 101 + round_id), 4) for round_id in range(ITERS)]
    return jnp.stack(order_rows, axis=0).astype(jnp.int32)


def with_ends(entries, own_key, low, largest):
    index_at = [jax.random.randint(jax.random.fold_in(own_key, axis), (), 0, length) for axis, length in enumerate(entries.shape)]
    longest = entries.shape.index(max(entries.shape))
    beside = index_at[:longest] + [(index_at[longest] + 1) % entries.shape[longest]] + index_at[longest + 1:]
    return entries.at[tuple(index_at)].set(low).at[tuple(beside)].set(largest)


def level_of(own_key, shape, cuts, low, top_value):
    factor_of = 1.0
    for axis_at, blocks in cuts:
        draws = jax.random.uniform(jax.random.fold_in(jax.random.fold_in(own_key, 6), axis_at), (blocks,), jnp.float32, low / len(cuts), top_value / len(cuts))
        factor_of = factor_of * jnp.repeat(jnp.exp(draws), shape[axis_at] // blocks).reshape((-1,) + (1,) * (len(shape) - 1 - axis_at))
    return factor_of


def bell_draw(own_key, extent, deviation, reach, shards=(), kind=jnp.bfloat16):
    drawn = jax.random.normal(own_key, extent, jnp.float32) * deviation
    if len(shards) > 0:
        drawn = level_of(own_key, extent, shards, -0.22, 0.18) * drawn
    return jnp.clip(drawn, min=-reach, max=reach).astype(kind)


def setup_inputs(seed: int = 0) -> dict:
    keys = jax.random.split(jax.random.key(seed), 11)
    return {
        "wind_speed": jnp.clip(jnp.exp(math.log(25.0) - 2.1202635 * jax.random.uniform(keys[0], (NX, NY), jnp.float32) ** level_of(keys[0], (NX, NY), ((0, 2), (1, 64)), -0.2, 0.2)), 3.0, 25.0),
        "wind_dir": jnp.clip(jax.random.uniform(keys[1], (NX, NY), jnp.float32, -3.140625, 3.140625), -3.140625, 3.140625),
        "depth_class": with_ends(jax.random.randint(keys[2], (NX, NY), 0, NCLASS), jax.random.fold_in(keys[2], 1), 0, NCLASS - 1).astype(jnp.int32),
        "group_speed": jnp.clip(jnp.exp(jax.random.uniform(keys[3], (NCLASS, NFREQ), jnp.float32, math.log(0.3), math.log(3.0))), 0.3, 3.0),
        "dissipation": jnp.clip(jnp.exp(jax.random.uniform(keys[4], (NCLASS, NFREQ), jnp.float32, math.log(0.02), math.log(1.0))), 0.02, 1.0),
        "input_rate": jnp.clip(jnp.exp(jax.random.uniform(keys[5], (NFREQ,), jnp.float32, math.log(0.02), math.log(0.2))), 0.02, 0.2),
        "outer_spectra": bell_draw(keys[6], (NPTS, K), 1.0, 6.0, ((0, 128),), jnp.float32),
        "dest_cell": draw_dest_cell(jax.random.fold_in(keys[10], 71), 0),
        "refraction_inverse": draw_refraction_inverse(jax.random.fold_in(keys[10], 71), 0),
        "sweep_order": draw_sweep_order(jax.random.fold_in(keys[10], 71), 0),
    }


whitecap_rate = 0.5


def reference(wind_speed, wind_dir, depth_class, group_speed, dissipation, input_rate, outer_spectra, dest_cell, refraction_inverse, sweep_order):
    angle = (jnp.arange(NDIR, dtype=jnp.float32) + 0.5) * (2.0 * math.pi / NDIR)
    cos_abs = jnp.abs(jnp.cos(angle))
    sin_abs = jnp.abs(jnp.sin(angle))
    quarter = NDIR // 4
    grid_row = dest_cell // NY
    grid_col = dest_cell % NY
    rim_slot = jnp.where(grid_row == 0, grid_col, jnp.where(grid_row == NX - 1, NY + grid_col, jnp.where(grid_col == 0, 2 * NY + grid_row, 2 * NY + NX + grid_row)))
    rim_sums = jax.ops.segment_sum(outer_spectra, rim_slot, num_segments=2 * NY + 2 * NX)
    top_row = rim_sums[:NY].T
    bottom_row = rim_sums[NY:2 * NY].T
    left_col = rim_sums[2 * NY:2 * NY + NX]
    right_col = rim_sums[2 * NY + NX:]
    classes = jnp.arange(NCLASS, dtype=jnp.int32)

    def sweep(state, quadrant):
        step_x = (1, -1, -1, 1)[quadrant]
        step_y = (1, 1, -1, -1)[quadrant]
        comp_low = quadrant * KQ
        comp_high = comp_low + KQ
        energy = jnp.mean(state * state, axis=0)
        previous = state[comp_low:comp_high]
        zero_col = jnp.zeros_like(previous[:, :, :1])
        if step_y == 1:
            beside = jnp.concatenate([zero_col, previous[:, :, :-1]], axis=2)
        else:
            beside = jnp.concatenate([previous[:, :, 1:], zero_col], axis=2)
        dir_cos = cos_abs[quadrant * quarter:(quadrant + 1) * quarter]
        dir_sin = sin_abs[quadrant * quarter:(quadrant + 1) * quarter]
        dir_angle = angle[quadrant * quarter:(quadrant + 1) * quarter]
        matrix = refraction_inverse[quadrant]

        def row_update(upwind, row_id):
            onehot = (depth_class[row_id][None, :] == classes[:, None]).astype(jnp.float32)
            speeds = jnp.sum(group_speed[:, :, None] * onehot[:, None, :], axis=0)
            losses = jnp.sum(dissipation[:, :, None] * onehot[:, None, :], axis=0)
            level = energy[row_id]
            damping = losses + whitecap_rate * level / (1.0 + level)
            along_x = dir_cos[:, None, None] * speeds[None]
            along_y = dir_sin[:, None, None] * speeds[None]
            denominator = (along_x + along_y + damping[None]).reshape(KQ, NY)
            spread = jnp.maximum(jnp.cos(dir_angle[:, None] - wind_dir[row_id][None, :]), 0.0)
            strength = (wind_speed[row_id] * 0.1) ** 2
            wind_input = (input_rate[None, :, None] * strength[None, None] * (spread * spread)[:, None]).reshape(KQ, NY)
            forcing = jnp.where(row_id == 0, top_row, 0.0) + jnp.where(row_id == NX - 1, bottom_row, 0.0)
            forcing = forcing.at[:, 0].add(left_col[row_id]).at[:, NY - 1].add(right_col[row_id])
            source = wind_input + forcing[comp_low:comp_high]
            known = along_y.reshape(KQ, NY) * beside[:, row_id] + source
            balance = (along_x.reshape(KQ, NY) * upwind + known) / denominator
            updated = jnp.dot(matrix, balance, precision=lax.Precision.HIGHEST, preferred_element_type=jnp.float32)
            return updated, updated

        final_row, new_rows = lax.scan(row_update, jnp.zeros((KQ, NY), jnp.float32), jnp.arange(NX, dtype=jnp.int32), reverse=(step_x == -1))
        return state.at[comp_low:comp_high].set(jnp.transpose(new_rows, (1, 0, 2)))

    branches = [lambda state, quad=quad: sweep(state, quad) for quad in range(4)]
    state = jnp.zeros((K, NX, NY), jnp.float32)
    for sweep_round in range(ITERS):
        for turn in range(4):
            state = lax.switch(sweep_order[sweep_round, turn], branches, state)
    return state
```

```python
from functools import partial
import math

import jax
import jax.numpy as jnp
import numpy as np
from jax import lax
from jax.experimental import pallas as pl
from jax.experimental.pallas import tpu as pltpu
from jax.sharding import PartitionSpec as P

NDIR = 36
NFREQ = 24
CAP = 16
ITERS = 2
QUARTER = NDIR // 4
KQ = QUARTER * NFREQ
KP = 256
K = 4 * KQ
KW = 896
ROWS = 16
HALF = 64
CW = 72

whitecap_rate = 0.5


def pack_kernel(source_ref, points_ref, cell_ref, out_ref, *tile_refs):
    count = points_ref.shape[0]
    for tile, tile_ref in enumerate(tile_refs[:-1]):
        tile_ref[...] = points_ref[:, tile * 128 : (tile + 1) * 128]
    tile_refs[-1][...] = jnp.concatenate(
        [
            points_ref[:, (len(tile_refs) - 1) * 128 :],
            jnp.broadcast_to(cell_ref[...], (count, KW - K)),
        ],
        axis=1,
    )
    sublane = lax.broadcasted_iota(jnp.int32, (8, 128), 0)

    def place(step, carry):
        tiles = [jnp.zeros((8, 128), jnp.float32)] * (KW // 128)
        for lane in range(8):
            source = source_ref[step * 8 + lane]
            chosen = sublane == jnp.where(source >= 0, lane, 8)
            point = jnp.maximum(source, 0)
            for tile, tile_ref in enumerate(tile_refs):
                row = tile_ref[pl.ds(point, 8, stride=0), :]
                tiles[tile] = jnp.where(chosen, row, tiles[tile])
        start = pl.multiple_of(step * 8, 8)
        for tile in range(KW // 128):
            out_ref[pl.ds(start, 8), pl.ds(tile * 128, 128)] = tiles[tile]
        return carry

    lax.fori_loop(0, out_ref.shape[0] // 8, place, 0)


def pack(source, points, cell, slots):
    return pl.pallas_call(
        pack_kernel,
        out_shape=jax.ShapeDtypeStruct((slots, KW), jnp.float32),
        in_specs=[
            pl.BlockSpec(memory_space=pltpu.SMEM),
            pl.BlockSpec(memory_space=pltpu.VMEM),
            pl.BlockSpec(memory_space=pltpu.VMEM),
        ],
        out_specs=pl.BlockSpec(memory_space=pltpu.VMEM),
        scratch_shapes=[pltpu.VMEM((points.shape[0], 128), jnp.float32)] * (KW // 128),
        compiler_params=pltpu.CompilerParams(vmem_limit_bytes=24 << 20),
        name="pack_points",
    )(source, points, cell)


def rim_forcing(outer_spectra, dest_cell, rows_dev, cols_dev):
    row_count = lax.axis_size("rows")
    col_count = lax.axis_size("cols")
    devices = row_count * col_count
    total_cols = cols_dev * col_count
    total_rows = rows_dev * row_count
    grid_row = dest_cell // total_cols
    grid_col = dest_cell % total_cols
    owner = grid_row // rows_dev * col_count + grid_col // cols_dev
    on_row = (grid_row == 0) | (grid_row == total_rows - 1)
    rim = jnp.where(on_row, grid_col % cols_dev, cols_dev + grid_row % rows_dev)
    position = jnp.arange(dest_cell.shape[0], dtype=jnp.int32)
    hot = owner[:, None] == jnp.arange(devices, dtype=jnp.int32)[None]
    before = (position[:, None] > position[None, :]).astype(jnp.bfloat16)
    earlier = jnp.dot(before, hot.astype(jnp.bfloat16), preferred_element_type=jnp.float32)
    rank = jnp.sum(jnp.where(hot, earlier, 0.0), axis=1).astype(jnp.int32)
    in_slot = rank[:, None] == jnp.arange(CAP, dtype=jnp.int32)[None]
    number = jnp.where(in_slot, (position + 1).astype(jnp.float32)[:, None], 0.0)
    source = lax.dot_general(
        hot.astype(jnp.float32),
        number,
        (((0,), (0,)), ((), ())),
        precision=lax.Precision.HIGHEST,
        preferred_element_type=jnp.float32,
    )
    source = source.astype(jnp.int32).reshape(-1) - 1
    outgoing = pack(source, outer_spectra, rim.astype(jnp.float32)[:, None], devices * CAP)
    arrived = lax.all_to_all(
        outgoing.reshape(devices, CAP, KW),
        ("rows", "cols"),
        split_axis=0,
        concat_axis=0,
        tiled=True,
    ).reshape(devices * CAP, KW)
    cells = arrived[:, K].astype(jnp.int32)
    rim_size = cols_dev + rows_dev
    member = (cells[:, None] == jnp.arange(rim_size, dtype=jnp.int32)[None]).astype(jnp.float32)
    return lax.dot_general(
        member,
        arrived[:, :K],
        (((0,), (0,)), ((), ())),
        precision=lax.Precision.HIGHEST,
        preferred_element_type=jnp.float32,
    )


def sweep_kernel(
    order_ref,
    wind_ref,
    speed_ref,
    loss_ref,
    rim_ref,
    side_ref,
    mask_ref,
    trig_ref,
    high_ref,
    low_ref,
    out_ref,
    state_ref,
    part_ref,
    total_ref,
    turned_ref,
    sem,
):
    total_ref[...] = jnp.zeros_like(total_ref)
    part_ref[...] = jnp.zeros_like(part_ref)

    def wide(x):
        return jnp.concatenate([x, x], axis=1)

    def one_sweep(iteration, turn):
        quad = order_ref[iteration, turn]
        up_x = (quad == 0) | (quad == 3)
        up_y = quad < 2
        cos_row = trig_ref[quad, 0:1, :]
        sin_row = trig_ref[quad, 1:2, :]
        both = cos_row + sin_row

        def row_of(s):
            return jnp.where(up_x, s, ROWS - 1 - s)

        def factors(s):
            row = row_of(s)
            speed = speed_ref[row]
            energy = total_ref[row] * (1.0 / K)
            damp = whitecap_rate * energy / (1.0 + energy)
            den = both * speed + loss_ref[row] + wide(damp)
            inv = 1.0 / den
            known = wind_ref[quad, row] + mask_ref[...] * side_ref[quad, row]
            if s == 0 or s == ROWS - 1:
                known = known + rim_ref[quad, jnp.where(row == 0, 0, 1)]
            if iteration > 0:
                old = state_ref[quad, row]
                beside = jnp.where(up_y, pltpu.roll(old, 1, 0), pltpu.roll(old, CW - 1, 0))
                known = known + sin_row * speed * beside
            return (cos_row * speed) * inv, known * inv

        copies = []
        nxt = factors(0)
        upwind = None
        for s in range(ROWS):
            along, fixed = nxt
            balance = fixed if s == 0 else along * upwind + fixed
            first = balance.astype(jnp.bfloat16)
            second = (balance - first.astype(jnp.float32)).astype(jnp.bfloat16)
            high = high_ref[quad]
            new = (
                jnp.dot(first, high, preferred_element_type=jnp.float32)
                + jnp.dot(second, high, preferred_element_type=jnp.float32)
                + jnp.dot(first, low_ref[quad], preferred_element_type=jnp.float32)
            )
            if s + 1 < ROWS:
                nxt = factors(s + 1)
            row = row_of(s)
            if iteration == 0:
                state_ref[quad, row] = new
            square = jnp.sum(new * new, axis=1, keepdims=True)
            square = jnp.broadcast_to(square, (CW, 128))
            total = (
                part_ref[(quad + 1) % 4, row]
                + part_ref[(quad + 2) % 4, row]
                + part_ref[(quad + 3) % 4, row]
                + square
            )
            part_ref[quad, row] = square
            total_ref[row] = total
            if iteration == ITERS - 1:
                own = new[:HALF]
                turned_ref[s] = jnp.concatenate([own, own], axis=0).T[:KQ]
                copy = pltpu.make_async_copy(
                    turned_ref.at[s],
                    out_ref.at[pl.ds(quad * KQ, KQ), row],
                    sem.at[s],
                )
                copy.start()
                copies.append(copy)
            upwind = new
        for copy in copies:
            copy.wait()

    for iteration in range(ITERS):

        def turn_body(turn, carry, iteration=iteration):
            one_sweep(iteration, turn)
            return carry

        lax.fori_loop(0, 4, turn_body, 0)


def run_sweeps(order, wind, speed, loss, rim, side, mask, trig, high, low):
    vmem = pl.BlockSpec(memory_space=pltpu.VMEM)
    return pl.pallas_call(
        sweep_kernel,
        out_shape=jax.ShapeDtypeStruct((K, ROWS, 128), jnp.float32),
        in_specs=[pl.BlockSpec(memory_space=pltpu.SMEM)] + [vmem] * 9,
        out_specs=pl.BlockSpec(memory_space=pl.ANY),
        scratch_shapes=[
            pltpu.VMEM((4, ROWS, CW, KP), jnp.float32),
            pltpu.VMEM((4, ROWS, CW, 128), jnp.float32),
            pltpu.VMEM((ROWS, CW, 128), jnp.float32),
            pltpu.VMEM((ROWS, KQ, 128), jnp.float32),
            pltpu.SemaphoreType.DMA((ROWS,)),
        ],
        compiler_params=pltpu.CompilerParams(vmem_limit_bytes=48 << 20),
        name="eight_sweeps",
    )(order, wind, speed, loss, rim, side, mask, trig, high, low)


def pad_quads(x, fill=0.0):
    parts = jnp.stack([x[..., q * KQ : (q + 1) * KQ] for q in range(4)], axis=0)
    pads = [(0, 0)] * (parts.ndim - 1) + [(0, KP - KQ)]
    return jnp.pad(parts, pads, constant_values=fill)


def with_halo(own, left, right):
    gap = jnp.zeros(own.shape[:-2] + (CW - HALF - 2, own.shape[-1]), own.dtype)
    return jnp.concatenate([own, right, gap, left], axis=-2)


def body(
    wind_speed,
    wind_dir,
    depth_class,
    group_speed,
    dissipation,
    input_rate,
    outer_spectra,
    dest_cell,
    refraction_inverse,
    sweep_order,
):
    rows_dev, cols_dev = wind_speed.shape
    col_count = lax.axis_size("cols")
    core = lax.axis_index("rows")
    chip = lax.axis_index("cols")
    swap = [(0, 1), (1, 0)]
    ahead = [(i, i + 1) for i in range(col_count - 1)]
    back = [(i + 1, i) for i in range(col_count - 1)]

    fields = jnp.stack([wind_speed, wind_dir, depth_class.astype(jnp.float32)], axis=-1)
    both = lax.all_gather(fields, "rows", axis=0, tiled=True)
    from_left = lax.ppermute(both[:, cols_dev - 1 :], "cols", ahead)
    from_right = lax.ppermute(both[:, :1], "cols", back)
    own = lax.dynamic_slice_in_dim(both, core * HALF, HALF, 1)
    left = jnp.where(core == 0, from_left, both[:, HALF - 1 : HALF])
    right = jnp.where(core == 0, both[:, HALF : HALF + 1], from_right)
    cells = with_halo(own, left, right)
    speed_in, dir_in, class_in = cells[..., 0:1], cells[..., 1:2], cells[..., 2:3]

    angle = (np.arange(NDIR, dtype=np.float64) + 0.5) * (2.0 * math.pi / NDIR)
    angle_k = np.repeat(angle, NFREQ).reshape(4, KQ)
    lanes = ((0, 0), (0, KP - KQ))
    cos_k = jnp.asarray(np.pad(np.cos(angle_k), lanes).astype(np.float32))
    sin_k = jnp.asarray(np.pad(np.sin(angle_k), lanes).astype(np.float32))
    trig = jnp.stack([jnp.abs(cos_k), jnp.abs(sin_k)], axis=1)
    rate_k = jnp.pad(jnp.tile(input_rate, QUARTER), (0, KP - KQ))
    strength = (speed_in * 0.1) ** 2
    spread = jnp.maximum(
        cos_k[:, None, None] * jnp.cos(dir_in)[None] + sin_k[:, None, None] * jnp.sin(dir_in)[None],
        0.0,
    )
    wind = (rate_k * strength)[None] * (spread * spread)

    def by_class(table, fill):
        wide = jnp.pad(
            jnp.tile(table, (1, QUARTER)), ((0, 0), (0, KP - KQ)), constant_values=fill
        )
        result = wide[0]
        for index in range(1, table.shape[0]):
            result = jnp.where(class_in == index, wide[index], result)
        return jnp.broadcast_to(result, (ROWS, CW, KP))

    speeds = by_class(group_speed, 0.0)
    losses = by_class(dissipation, 1.0)
    matrix = jnp.pad(
        jnp.swapaxes(refraction_inverse, 1, 2), ((0, 0), (0, KP - KQ), (0, KP - KQ))
    )
    rounded = lax.reduce_precision(matrix, 8, 7)
    high = rounded.astype(jnp.bfloat16)
    low = (matrix - rounded).astype(jnp.bfloat16)

    rim = rim_forcing(outer_spectra, dest_cell, rows_dev, cols_dev)
    near = lax.dynamic_slice_in_dim(rim, core * HALF, HALF, 0)
    edge = jnp.where(core == 0, rim[HALF : HALF + 1], rim[HALF - 1 : HALF])
    far = lax.dynamic_slice_in_dim(rim, (1 - core) * HALF, HALF, 0)
    far_edge = jnp.where(core == 0, rim[HALF - 1 : HALF], rim[HALF : HALF + 1])
    side = rim[cols_dev:]
    got = lax.ppermute(jnp.concatenate([far, side, far_edge], axis=0), "rows", swap)
    first, last = rim[:1], rim[cols_dev - 1 : cols_dev]

    def flat(row, col):
        return row * col_count + col

    straight = [(flat(0, c), flat(0, c + 1)) for c in range(col_count - 1)]
    straight += [(flat(1, c), flat(1, c - 1)) for c in range(1, col_count)]
    across = [(flat(1, c), flat(0, c + 1)) for c in range(col_count - 1)]
    across += [(flat(0, c), flat(1, c - 1)) for c in range(1, col_count)]
    mine_out = lax.ppermute(jnp.where(core == 0, last, first), ("rows", "cols"), straight)
    other_out = lax.ppermute(jnp.where(core == 0, first, last), ("rows", "cols"), across)

    def rim_row(inner, outer, columns):
        lefts = jnp.where(core == 0, outer, inner)
        rights = jnp.where(core == 0, inner, outer)
        return with_halo(columns, lefts, rights)

    mine = rim_row(edge, mine_out, near)
    other = rim_row(got[HALF + rows_dev :], other_out, got[:HALF])
    top = jnp.where(core == 0, mine, other)
    bottom = jnp.where(core == 0, other, mine)
    rim_rows = pad_quads(jnp.stack([top, bottom], axis=0))
    other_side = got[HALF : HALF + rows_dev]
    sides = jnp.where(
        core == 0,
        jnp.concatenate([side, other_side], axis=0),
        jnp.concatenate([other_side, side], axis=0),
    )
    side_rows = pad_quads(sides[:, None, :])
    at_col = jnp.where(
        (chip == 0) & (core == 0),
        0,
        jnp.where((chip == col_count - 1) & (core == 1), HALF - 1, CW),
    )
    mask = (jnp.arange(CW, dtype=jnp.int32) == at_col).astype(jnp.float32)
    mask = jnp.broadcast_to(mask[:, None], (CW, KP))

    out = run_sweeps(
        sweep_order, wind, speeds, losses, rim_rows, side_rows, mask, trig, high, low
    )
    keep = lax.dynamic_slice_in_dim(out, core * rows_dev, rows_dev, 1)
    give = lax.dynamic_slice_in_dim(out, (1 - core) * rows_dev, rows_dev, 1)
    taken = lax.ppermute(give, "rows", swap)
    lane_core = jnp.arange(cols_dev, dtype=jnp.int32) // HALF
    return jnp.where(lane_core == core, keep, taken)


def solution(mesh):
    placed = (
        P("rows", "cols"),
        P("rows", "cols"),
        P("rows", "cols"),
        P(),
        P(),
        P(),
        P(("rows", "cols"), None),
        P(("rows", "cols")),
        P(),
        P(),
    )
    return jax.shard_map(
        body, mesh=mesh, in_specs=placed, out_specs=P(None, "rows", "cols"), check_vma=False
    )
```

```python
from functools import partial
import math

import jax
import jax.numpy as jnp
import numpy as np
from jax import lax
from jax.experimental import pallas as pl
from jax.experimental.pallas import tpu as pltpu
from jax.sharding import PartitionSpec as P

NDIR = 36
NFREQ = 24
CAP = 16
ITERS = 2
QUARTER = NDIR // 4
KQ = QUARTER * NFREQ
KP = 256
K = 4 * KQ
TILES = 7
WIDE = 124
CELLS = 144
ROWS = 16
HALF = 64
CW = 72

whitecap_rate = 0.5


def place_of(order, dest):
    at = (dest % 4, dest // 4 % 4, dest // 16)
    return at[order] * 16 + at[(order + 1) % 3] * 4 + at[(order + 2) % 3]


def pack_kernel(source_ref, points_ref, cell_ref, out_ref, load_ref, done_ref, *rest):
    tile_refs, (load_sem, done_sem) = rest[:TILES], rest[TILES:]
    count = points_ref.shape[0]
    part = count // 4
    loads = []
    for step in range(4):
        rows = pl.ds(step * part, part)
        load = pltpu.make_async_copy(points_ref.at[rows], load_ref.at[rows], load_sem.at[step])
        load.start()
        loads.append(load)
    for step in range(4):
        loads[step].wait()
        rows = pl.ds(step * part, part)
        ids = jnp.broadcast_to(cell_ref[rows], (part, 128 - WIDE))
        for tile, tile_ref in enumerate(tile_refs):
            low = tile * WIDE
            high = min(low + WIDE, K)
            pieces = [load_ref[rows, low:high]]
            if high - low < WIDE:
                pieces.append(jnp.zeros((part, WIDE - high + low), jnp.float32))
            tile_ref[rows] = jnp.concatenate(pieces + [ids], axis=1)
    sublane = lax.broadcasted_iota(jnp.int32, (8, 128), 0)
    saves = []
    for row in range(2):

        def place(step, carry, row=row):
            tiles = [jnp.zeros((8, 128), jnp.float32)] * TILES
            for lane in range(8):
                source = source_ref[row * 1024 + step * 8 + lane]
                chosen = sublane == jnp.where(source >= 0, lane, 8)
                point = jnp.maximum(source, 0)
                for tile, tile_ref in enumerate(tile_refs):
                    found = tile_ref[pl.ds(point, 8, stride=0), :]
                    tiles[tile] = jnp.where(chosen, found, tiles[tile])
            dest = step // 2
            half = step % 2 * 8
            starts = [place_of(order, dest) * CAP + half for order in range(3)]
            for tile in range(TILES):
                start = pl.multiple_of(starts[(tile + row) % 3], 8)
                done_ref[row, tile, pl.ds(start, 8), :] = tiles[tile]
            return carry

        lax.fori_loop(0, 128, place, 0)
        save = pltpu.make_async_copy(done_ref.at[row], out_ref.at[row], done_sem.at[row])
        save.start()
        saves.append(save)
    for save in saves:
        save.wait()


def pack(source, points, cell):
    return pl.pallas_call(
        pack_kernel,
        out_shape=jax.ShapeDtypeStruct((2, TILES, 1024, 128), jnp.float32),
        in_specs=[
            pl.BlockSpec(memory_space=pltpu.SMEM),
            pl.BlockSpec(memory_space=pl.ANY),
            pl.BlockSpec(memory_space=pltpu.VMEM),
        ],
        out_specs=pl.BlockSpec(memory_space=pl.ANY),
        scratch_shapes=[
            pltpu.VMEM(points.shape, jnp.float32),
            pltpu.VMEM((2, TILES, 1024, 128), jnp.float32),
        ]
        + [pltpu.VMEM((points.shape[0], 128), jnp.float32)] * TILES
        + [pltpu.SemaphoreType.DMA((4,)), pltpu.SemaphoreType.DMA((2,))],
        compiler_params=pltpu.CompilerParams(vmem_limit_bytes=32 << 20),
        name="pack_points",
    )(source, points, cell)


def exchange_kernel(
    slots_ref,
    rim_ref,
    side_ref,
    near_ref,
    far_ref,
    hot_ref,
    dense_ref,
    last_ref,
    own_ref,
    other_ref,
    edge_ref,
    send1,
    recv1,
    send2,
    recv2,
    send3,
    recv3,
    send4,
    recv4,
):
    core = lax.axis_index("rows")
    chip = lax.axis_index("cols")
    strides = (1, 4, 16)
    at = tuple(chip // stride % 4 for stride in strides)
    chips = 64

    def moved(axis, value):
        return chip + (value - at[axis]) * strides[axis]

    def remote(src, dst, send, recv, row, col):
        return pltpu.make_async_remote_copy(
            src_ref=src,
            dst_ref=dst,
            send_sem=send,
            recv_sem=recv,
            device_id=(row, col),
            device_id_type=pl.DeviceIdType.MESH,
        )

    def drain(ref, sem):
        pltpu.make_async_copy(ref, ref, sem).wait()

    barrier = pltpu.get_barrier_semaphore()

    def greet(row, col):
        pl.semaphore_signal(
            barrier, inc=1, device_id=(row, col), device_id_type=pl.DeviceIdType.MESH
        )

    for axis in range(3):
        for step in range(1, 4):
            for row in range(2):
                greet(row, moved(axis, (at[axis] + step) % 4))
    greet(1 - core, chip)

    after, before = (chip + 1) % chips, (chip + chips - 1) % chips
    greet(0, after)
    greet(1, before)
    greet(core, (chip + chips - 1 + 2 * core) % chips)
    pl.semaphore_wait(barrier, 22)

    for tile in range(TILES):
        for row in range(2):
            axis = (tile + row) % 3
            mine = core * 4 + at[axis]
            for step in range(1, 4):
                goal = (at[axis] + step) % 4
                remote(
                    slots_ref.at[row, tile, pl.ds(pl.multiple_of(goal * 256, 256), 256)],
                    near_ref.at[tile, mine],
                    send1.at[tile],
                    recv1.at[tile],
                    row,
                    moved(axis, goal),
                ).start()
            rest = slots_ref.at[row, tile, pl.ds(pl.multiple_of(at[axis] * 256, 256), 256)]

            @pl.when(core != row)
            def _():
                remote(
                    rest, near_ref.at[tile, mine], send1.at[tile], recv1.at[tile], row, chip
                ).start()

            @pl.when(core == row)
            def _():
                pltpu.make_async_copy(rest, near_ref.at[tile, mine], recv1.at[tile]).start()

    def axis_of(tile, turn):
        even = (tile + turn) % 3
        odd = (tile + 1 + turn) % 3
        place = (1 - core) * at[even] + core * at[odd]
        stride = (1 - core) * strides[even] + core * strides[odd]
        return place, stride

    for tile in range(TILES):
        drain(near_ref.at[tile], recv1.at[tile])
        place, stride = axis_of(tile, 1)
        for step in range(1, 4):
            goal = (place + step) % 4
            remote(
                near_ref.at[tile, :, pl.ds(pl.multiple_of(goal * 64, 64), 64)],
                far_ref.at[tile, place],
                send2.at[tile],
                recv2.at[tile],
                core,
                chip + (goal - place) * stride,
            ).start()
        pltpu.make_async_copy(
            near_ref.at[tile, :, pl.ds(pl.multiple_of(place * 64, 64), 64)],
            far_ref.at[tile, place],
            recv2.at[tile],
        ).start()

    cell = lax.broadcasted_iota(jnp.int32, (CELLS, 512), 0)
    for tile in range(TILES):
        drain(far_ref.at[tile], recv2.at[tile])
        for goal in range(4):
            slab = far_ref[tile, :, :, goal * CAP : (goal + 1) * CAP, :].reshape(512, 128)
            if tile < 3:
                ids = slab.T[127:128, :].astype(jnp.int32)
                hot_ref[tile, goal] = jnp.where(cell == ids, 1.0, 0.0).astype(jnp.bfloat16)
            member = hot_ref[tile % 3, goal]
            first = slab.astype(jnp.bfloat16)
            second = (slab - first.astype(jnp.float32)).astype(jnp.bfloat16)
            dense_ref[tile, goal] = jnp.dot(
                member, first, preferred_element_type=jnp.float32
            ) + jnp.dot(member, second, preferred_element_type=jnp.float32)
        place, stride = axis_of(tile, 2)
        for step in range(1, 4):
            goal = (place + step) % 4
            remote(
                dense_ref.at[tile, goal],
                last_ref.at[tile, place],
                send3.at[tile],
                recv3.at[tile],
                core,
                chip + (goal - place) * stride,
            ).start()
        pltpu.make_async_copy(
            dense_ref.at[tile, place], last_ref.at[tile, place], recv3.at[tile]
        ).start()
    for tile in range(TILES):
        drain(last_ref.at[tile], recv3.at[tile])
        own_ref[tile] = (
            last_ref[tile, 0] + last_ref[tile, 1] + last_ref[tile, 2] + last_ref[tile, 3]
        )

    swap = remote(own_ref, other_ref, send4.at[0], recv4.at[0], 1 - core, chip)
    swap.start()
    right = remote(
        own_ref.at[:, pl.ds(120, 8)], edge_ref.at[core], send4.at[1], recv4.at[1 + core], 0, after
    )
    right.start()
    left = remote(
        own_ref.at[:, pl.ds(0, 8)], edge_ref.at[core], send4.at[2], recv4.at[1 + core], 1, before
    )
    left.start()
    swap.wait()
    for row in range(2):
        drain(edge_ref.at[row], recv4.at[1 + row])
    right.wait_send()
    left.wait_send()
    outside = jnp.where(core == 0, chip == 0, chip == chips - 1)
    inside = jnp.where(outside, 0.0, 1.0)

    def quads(tiles):
        full = jnp.concatenate([part[:, :WIDE] for part in tiles], axis=1)
        gap = jnp.zeros((full.shape[0], KP - KQ), jnp.float32)
        return [
            jnp.concatenate([full[:, q * KQ : (q + 1) * KQ], gap], axis=1) for q in range(4)
        ]

    gap = jnp.zeros((6, 128), jnp.float32)
    mine = pl.ds(pl.multiple_of(core * HALF, HALF), HALF)
    for row in range(2):
        tiles = []
        sides = []
        for tile in range(TILES):
            own, other = own_ref[tile, mine, :], other_ref[tile, mine, :]
            columns = jnp.where(core == row, own, other)
            low = jnp.where(core == row, own_ref[tile, 56:72, :], other_ref[tile, 56:72, :])
            edge = edge_ref[row, tile] * inside
            rights = jnp.where(core == 0, low[8:9], edge[0:1])
            lefts = jnp.where(core == 0, edge[7:8], low[7:8])
            tiles.append(jnp.concatenate([columns, rights, gap, lefts], axis=0))
            sides.append(
                jnp.where(core == row, own_ref[tile, 128:136, :], other_ref[tile, 128:136, :])
            )
        for quad, value in enumerate(quads(tiles)):
            rim_ref[quad, row] = value
        for quad, value in enumerate(quads(sides)):
            for index in range(8):
                side_ref[quad, row * 8 + index] = value[index : index + 1]

    for tile in range(TILES):
        drain(near_ref.at[tile, pl.ds(0, 7)], send1.at[tile])
        drain(far_ref.at[tile, pl.ds(0, 3)], send2.at[tile])
        drain(last_ref.at[tile, pl.ds(0, 3)], send3.at[tile])


def exchange(slots):
    dma = pltpu.SemaphoreType.DMA
    vmem = pl.BlockSpec(memory_space=pltpu.VMEM)
    return pl.pallas_call(
        exchange_kernel,
        out_shape=(
            jax.ShapeDtypeStruct((4, 2, CW, KP), jnp.float32),
            jax.ShapeDtypeStruct((4, ROWS, 1, KP), jnp.float32),
        ),
        in_specs=[pl.BlockSpec(memory_space=pl.ANY)],
        out_specs=(vmem, vmem),
        scratch_shapes=[
            pltpu.VMEM((TILES, 8, 256, 128), jnp.float32),
            pltpu.VMEM((TILES, 4, 8, 64, 128), jnp.float32),
            pltpu.VMEM((3, 4, CELLS, 512), jnp.bfloat16),
            pltpu.VMEM((TILES, 4, CELLS, 128), jnp.float32),
            pltpu.VMEM((TILES, 4, CELLS, 128), jnp.float32),
            pltpu.VMEM((TILES, CELLS, 128), jnp.float32),
            pltpu.VMEM((TILES, CELLS, 128), jnp.float32),
            pltpu.VMEM((2, TILES, 8, 128), jnp.float32),
            dma((TILES,)),
            dma((TILES,)),
            dma((TILES,)),
            dma((TILES,)),
            dma((TILES,)),
            dma((TILES,)),
            dma((3,)),
            dma((3,)),
        ],
        compiler_params=pltpu.CompilerParams(
            vmem_limit_bytes=40 << 20, collective_id=0, has_side_effects=True
        ),
        name="exchange_points",
    )(slots)


def rim_forcing(outer_spectra, dest_cell, rows_dev, cols_dev):
    row_count = lax.axis_size("rows")
    col_count = lax.axis_size("cols")
    devices = row_count * col_count
    total_cols = cols_dev * col_count
    total_rows = rows_dev * row_count
    grid_row = dest_cell // total_cols
    grid_col = dest_cell % total_cols
    owner = grid_row // rows_dev * col_count + grid_col // cols_dev
    on_row = (grid_row == 0) | (grid_row == total_rows - 1)
    rim = jnp.where(on_row, grid_col % cols_dev, cols_dev + grid_row % rows_dev)
    position = jnp.arange(dest_cell.shape[0], dtype=jnp.int32)
    hot = owner[:, None] == jnp.arange(devices, dtype=jnp.int32)[None]
    before = (position[:, None] > position[None, :]).astype(jnp.bfloat16)
    earlier = jnp.dot(before, hot.astype(jnp.bfloat16), preferred_element_type=jnp.float32)
    rank = jnp.sum(jnp.where(hot, earlier, 0.0), axis=1).astype(jnp.int32)
    in_slot = rank[:, None] == jnp.arange(CAP, dtype=jnp.int32)[None]
    number = jnp.where(in_slot, (position + 1).astype(jnp.float32)[:, None], 0.0)
    source = lax.dot_general(
        hot.astype(jnp.float32),
        number,
        (((0,), (0,)), ((), ())),
        precision=lax.Precision.HIGHEST,
        preferred_element_type=jnp.float32,
    )
    source = source.astype(jnp.int32).reshape(-1) - 1
    slots = pack(source, outer_spectra, rim.astype(jnp.float32)[:, None])
    return exchange(slots)


def sweep_kernel(
    order_ref,
    wind_ref,
    speed_ref,
    loss_ref,
    rim_ref,
    side_ref,
    mask_ref,
    trig_ref,
    high_ref,
    low_ref,
    out_ref,
    state_ref,
    part_ref,
    total_ref,
    turned_ref,
    sem,
):
    total_ref[...] = jnp.zeros_like(total_ref)
    part_ref[...] = jnp.zeros_like(part_ref)

    def wide(x):
        return jnp.concatenate([x, x], axis=1)

    def one_sweep(iteration, turn):
        quad = order_ref[iteration, turn]
        up_x = (quad == 0) | (quad == 3)
        up_y = quad < 2
        cos_row = trig_ref[quad, 0:1, :]
        sin_row = trig_ref[quad, 1:2, :]
        both = cos_row + sin_row

        def row_of(s):
            return jnp.where(up_x, s, ROWS - 1 - s)

        def factors(s):
            row = row_of(s)
            speed = speed_ref[row]
            energy = total_ref[row] * (1.0 / K)
            damp = whitecap_rate * energy / (1.0 + energy)
            den = both * speed + loss_ref[row] + wide(damp)
            inv = 1.0 / den
            known = wind_ref[quad, row] + mask_ref[...] * side_ref[quad, row]
            if s == 0 or s == ROWS - 1:
                known = known + rim_ref[quad, jnp.where(row == 0, 0, 1)]
            if iteration > 0:
                old = state_ref[quad, row]
                beside = jnp.where(up_y, pltpu.roll(old, 1, 0), pltpu.roll(old, CW - 1, 0))
                known = known + sin_row * speed * beside
            return (cos_row * speed) * inv, known * inv

        copies = []
        nxt = factors(0)
        upwind = None
        for s in range(ROWS):
            along, fixed = nxt
            balance = fixed if s == 0 else along * upwind + fixed
            first = balance.astype(jnp.bfloat16)
            second = (balance - first.astype(jnp.float32)).astype(jnp.bfloat16)
            high = high_ref[quad]
            new = (
                jnp.dot(first, high, preferred_element_type=jnp.float32)
                + jnp.dot(second, high, preferred_element_type=jnp.float32)
                + jnp.dot(first, low_ref[quad], preferred_element_type=jnp.float32)
            )
            if s + 1 < ROWS:
                nxt = factors(s + 1)
            row = row_of(s)
            if iteration == 0:
                state_ref[quad, row] = new
            square = jnp.sum(new * new, axis=1, keepdims=True)
            square = jnp.broadcast_to(square, (CW, 128))
            total = (
                part_ref[(quad + 1) % 4, row]
                + part_ref[(quad + 2) % 4, row]
                + part_ref[(quad + 3) % 4, row]
                + square
            )
            part_ref[quad, row] = square
            total_ref[row] = total
            if iteration == ITERS - 1:
                own = new[:HALF]
                turned_ref[s] = jnp.concatenate([own, own], axis=0).T[:KQ]
                copy = pltpu.make_async_copy(
                    turned_ref.at[s],
                    out_ref.at[pl.ds(quad * KQ, KQ), row],
                    sem.at[s],
                )
                copy.start()
                copies.append(copy)
            upwind = new
        for copy in copies:
            copy.wait()

    for iteration in range(ITERS):

        def turn_body(turn, carry, iteration=iteration):
            one_sweep(iteration, turn)
            return carry

        lax.fori_loop(0, 4, turn_body, 0)


def run_sweeps(order, wind, speed, loss, rim, side, mask, trig, high, low):
    vmem = pl.BlockSpec(memory_space=pltpu.VMEM)
    return pl.pallas_call(
        sweep_kernel,
        out_shape=jax.ShapeDtypeStruct((K, ROWS, 128), jnp.float32),
        in_specs=[pl.BlockSpec(memory_space=pltpu.SMEM)] + [vmem] * 9,
        out_specs=pl.BlockSpec(memory_space=pl.ANY),
        scratch_shapes=[
            pltpu.VMEM((4, ROWS, CW, KP), jnp.float32),
            pltpu.VMEM((4, ROWS, CW, 128), jnp.float32),
            pltpu.VMEM((ROWS, CW, 128), jnp.float32),
            pltpu.VMEM((ROWS, KQ, 128), jnp.float32),
            pltpu.SemaphoreType.DMA((ROWS,)),
        ],
        compiler_params=pltpu.CompilerParams(vmem_limit_bytes=48 << 20),
        name="eight_sweeps",
    )(order, wind, speed, loss, rim, side, mask, trig, high, low)


def with_halo(own, left, right):
    gap = jnp.zeros(own.shape[:-2] + (CW - HALF - 2, own.shape[-1]), own.dtype)
    return jnp.concatenate([own, right, gap, left], axis=-2)


def body(
    wind_speed,
    wind_dir,
    depth_class,
    group_speed,
    dissipation,
    input_rate,
    outer_spectra,
    dest_cell,
    refraction_inverse,
    sweep_order,
):
    rows_dev, cols_dev = wind_speed.shape
    col_count = lax.axis_size("cols")
    core = lax.axis_index("rows")
    chip = lax.axis_index("cols")
    swap = [(0, 1), (1, 0)]
    ahead = [(i, i + 1) for i in range(col_count - 1)]
    back = [(i + 1, i) for i in range(col_count - 1)]

    fields = jnp.stack([wind_speed, wind_dir, depth_class.astype(jnp.float32)], axis=-1)
    both = lax.all_gather(fields, "rows", axis=0, tiled=True)
    from_left = lax.ppermute(both[:, cols_dev - 1 :], "cols", ahead)
    from_right = lax.ppermute(both[:, :1], "cols", back)
    own = lax.dynamic_slice_in_dim(both, core * HALF, HALF, 1)
    left = jnp.where(core == 0, from_left, both[:, HALF - 1 : HALF])
    right = jnp.where(core == 0, both[:, HALF : HALF + 1], from_right)
    cells = with_halo(own, left, right)
    speed_in, dir_in, class_in = cells[..., 0:1], cells[..., 1:2], cells[..., 2:3]

    angle = (np.arange(NDIR, dtype=np.float64) + 0.5) * (2.0 * math.pi / NDIR)
    angle_k = np.repeat(angle, NFREQ).reshape(4, KQ)
    lanes = ((0, 0), (0, KP - KQ))
    cos_k = jnp.asarray(np.pad(np.cos(angle_k), lanes).astype(np.float32))
    sin_k = jnp.asarray(np.pad(np.sin(angle_k), lanes).astype(np.float32))
    trig = jnp.stack([jnp.abs(cos_k), jnp.abs(sin_k)], axis=1)
    rate_k = jnp.pad(jnp.tile(input_rate, QUARTER), (0, KP - KQ))
    strength = (speed_in * 0.1) ** 2
    spread = jnp.maximum(
        cos_k[:, None, None] * jnp.cos(dir_in)[None] + sin_k[:, None, None] * jnp.sin(dir_in)[None],
        0.0,
    )
    wind = (rate_k * strength)[None] * (spread * spread)

    def by_class(table, fill):
        wide = jnp.pad(
            jnp.tile(table, (1, QUARTER)), ((0, 0), (0, KP - KQ)), constant_values=fill
        )
        result = wide[0]
        for index in range(1, table.shape[0]):
            result = jnp.where(class_in == index, wide[index], result)
        return jnp.broadcast_to(result, (ROWS, CW, KP))

    speeds = by_class(group_speed, 0.0)
    losses = by_class(dissipation, 1.0)
    matrix = jnp.pad(
        jnp.swapaxes(refraction_inverse, 1, 2), ((0, 0), (0, KP - KQ), (0, KP - KQ))
    )
    rounded = lax.reduce_precision(matrix, 8, 7)
    high = rounded.astype(jnp.bfloat16)
    low = (matrix - rounded).astype(jnp.bfloat16)

    rim_rows, side_rows = rim_forcing(outer_spectra, dest_cell, rows_dev, cols_dev)
    at_col = jnp.where(
        (chip == 0) & (core == 0),
        0,
        jnp.where((chip == col_count - 1) & (core == 1), HALF - 1, CW),
    )
    mask = (jnp.arange(CW, dtype=jnp.int32) == at_col).astype(jnp.float32)
    mask = jnp.broadcast_to(mask[:, None], (CW, KP))

    out = run_sweeps(
        sweep_order, wind, speeds, losses, rim_rows, side_rows, mask, trig, high, low
    )
    keep = lax.dynamic_slice_in_dim(out, core * rows_dev, rows_dev, 1)
    give = lax.dynamic_slice_in_dim(out, (1 - core) * rows_dev, rows_dev, 1)
    taken = lax.ppermute(give, "rows", swap)
    lane_core = jnp.arange(cols_dev, dtype=jnp.int32) // HALF
    return jnp.where(lane_core == core, keep, taken)


def solution(mesh):
    placed = (
        P("rows", "cols"),
        P("rows", "cols"),
        P("rows", "cols"),
        P(),
        P(),
        P(),
        P(("rows", "cols"), None),
        P(("rows", "cols")),
        P(),
        P(),
    )
    return jax.shard_map(
        body, mesh=mesh, in_specs=placed, out_specs=P(None, "rows", "cols"), check_vma=False
    )
```

```python
from functools import partial
import math

import jax
import jax.numpy as jnp
import numpy as np
from jax import lax
from jax.experimental import pallas as pl
from jax.experimental.pallas import tpu as pltpu
from jax.sharding import PartitionSpec as P

NDIR = 36
NFREQ = 24
CAP = 16
ITERS = 2
QUARTER = NDIR // 4
KQ = QUARTER * NFREQ
KP = 256
K = 4 * KQ
TILES = 7
WIDE = 124
CELLS = 144
ROWS = 16
HALF = 64
CW = 72

whitecap_rate = 0.5


def place_of(order, dest):
    at = (dest % 4, dest // 4 % 4, dest // 16)
    return at[order] * 16 + at[(order + 1) % 3] * 4 + at[(order + 2) % 3]


def exchange_kernel(
    source_ref,
    points_ref,
    id_ref,
    speed_ref,
    dir_ref,
    class_ref,
    rim_ref,
    side_ref,
    cols_ref,
    load_ref,
    stage_ref,
    slots_ref,
    near_ref,
    far_ref,
    hot_ref,
    dense_ref,
    last_ref,
    own_ref,
    other_ref,
    edge_ref,
    field_ref,
    field_other_ref,
    field_edge_ref,
    turn_ref,
    load_sem,
    send1,
    recv1,
    send2,
    recv2,
    send3,
    recv3,
    send4,
    recv4,
    send5,
    recv5,
):
    core = lax.axis_index("rows")
    chip = lax.axis_index("cols")
    strides = (1, 4, 16)
    at = tuple(chip // stride % 4 for stride in strides)
    chips = 64

    def moved(axis, value):
        return chip + (value - at[axis]) * strides[axis]

    def remote(src, dst, send, recv, row, col):
        return pltpu.make_async_remote_copy(
            src_ref=src,
            dst_ref=dst,
            send_sem=send,
            recv_sem=recv,
            device_id=(row, col),
            device_id_type=pl.DeviceIdType.MESH,
        )

    def drain(ref, sem):
        pltpu.make_async_copy(ref, ref, sem).wait()

    count = points_ref.shape[0]
    part = count // 4
    loads = []
    for step in range(4):
        rows = pl.ds(step * part, part)
        load = pltpu.make_async_copy(points_ref.at[rows], load_ref.at[rows], load_sem.at[step])
        load.start()
        loads.append(load)
    field_ref[0:8] = speed_ref[...]
    field_ref[8:16] = dir_ref[...]
    field_ref[16:24] = class_ref[...].astype(jnp.float32)

    barrier = pltpu.get_barrier_semaphore()

    def greet(row, col):
        pl.semaphore_signal(
            barrier, inc=1, device_id=(row, col), device_id_type=pl.DeviceIdType.MESH
        )

    for axis in range(3):
        for step in range(1, 4):
            for row in range(2):
                greet(row, moved(axis, (at[axis] + step) % 4))
    greet(1 - core, chip)

    after, before = (chip + 1) % chips, (chip + chips - 1) % chips
    greet(0, after)
    greet(1, before)
    greet(core, (chip + chips - 1 + 2 * core) % chips)
    pl.semaphore_wait(barrier, 22)

    trades = []
    for index, (row, col) in enumerate(((1 - core, chip), (0, after), (1, before))):
        goal_ref = field_other_ref if index == 0 else field_edge_ref.at[core]
        arrival = recv5.at[0] if index == 0 else recv5.at[1 + core]
        trade = remote(field_ref, goal_ref, send5.at[index], arrival, row, col)
        trade.start()
        trades.append(trade)

    sublane = lax.broadcasted_iota(jnp.int32, (8, 128), 0)
    for load in loads:
        load.wait()
    ids = jnp.broadcast_to(id_ref[...], (count, 128 - WIDE))
    for group in ((0,), (1, 2), (3, 4), (5, 6)):
        for tile in group:
            low = tile * WIDE
            high = min(low + WIDE, K)
            pieces = [load_ref[:, low:high]]
            if high - low < WIDE:
                pieces.append(jnp.zeros((count, WIDE - high + low), jnp.float32))
            stage_ref[tile, 0:count] = jnp.concatenate(pieces + [ids], axis=1)
            stage_ref[tile, count:] = jnp.zeros((8, 128), jnp.float32)
        for row in range(2):

            def place(dest, carry, row=row, group=group):
                starts = [place_of((tile + row) % 3, dest) * CAP for tile in group]
                for half in range(2):
                    tiles = [None] * len(group)
                    for lane in range(8):
                        point = source_ref[row * 1024 + dest * CAP + half * 8 + lane]
                        for index, tile in enumerate(group):
                            found = stage_ref.at[tile][pl.ds(point, 8, stride=0), :]
                            tiles[index] = (
                                found
                                if lane == 0
                                else jnp.where(sublane == lane, found, tiles[index])
                            )
                    for index, tile in enumerate(group):
                        start = pl.multiple_of(starts[index] + half * 8, 8)
                        slots_ref[row, tile, pl.ds(start, 8), :] = tiles[index]
                return carry

            lax.fori_loop(0, 64, place, 0)
        for tile in group:
            for row in range(2):
                axis = (tile + row) % 3
                mine = core * 4 + at[axis]
                for step in range(1, 4):
                    goal = (at[axis] + step) % 4
                    remote(
                        slots_ref.at[row, tile, pl.ds(pl.multiple_of(goal * 256, 256), 256)],
                        near_ref.at[tile, mine],
                        send1.at[tile],
                        recv1.at[tile],
                        row,
                        moved(axis, goal),
                    ).start()
                rest = slots_ref.at[row, tile, pl.ds(pl.multiple_of(at[axis] * 256, 256), 256)]

                @pl.when(core != row)
                def _():
                    remote(
                        rest, near_ref.at[tile, mine], send1.at[tile], recv1.at[tile], row, chip
                    ).start()

                @pl.when(core == row)
                def _():
                    pltpu.make_async_copy(rest, near_ref.at[tile, mine], recv1.at[tile]).start()

    outside = jnp.where(core == 0, chip == 0, chip == chips - 1)
    inside = jnp.where(outside, 0.0, 1.0)
    for trade in trades:
        trade.wait_send()
    drain(field_other_ref, recv5.at[0])
    for row in range(2):
        drain(field_edge_ref.at[row], recv5.at[1 + row])
    own_field, other_field = field_ref[...], field_other_ref[...]
    pad = jnp.zeros((80, 128), jnp.float32)
    both = [jnp.where(core == row, own_field, other_field) for row in range(2)]
    turn_ref[...] = jnp.concatenate(both + [pad], axis=0).T
    edges = jnp.concatenate([field_edge_ref[0], field_edge_ref[1], pad], axis=0).T * inside
    middle = turn_ref[56:72]
    mine = pl.ds(pl.multiple_of(core * HALF, HALF), HALF)
    gap = jnp.zeros((6, 128), jnp.float32)
    cols_ref[...] = jnp.concatenate(
        [
            turn_ref[mine],
            jnp.where(core == 0, middle[8:9], edges[0:1]),
            gap,
            jnp.where(core == 0, edges[127:128], middle[7:8]),
        ],
        axis=0,
    )

    def axis_of(tile, turn):
        even = (tile + turn) % 3
        odd = (tile + 1 + turn) % 3
        place = (1 - core) * at[even] + core * at[odd]
        stride = (1 - core) * strides[even] + core * strides[odd]
        return place, stride

    for tile in range(TILES):
        drain(near_ref.at[tile], recv1.at[tile])
        place, stride = axis_of(tile, 1)
        for step in range(1, 4):
            goal = (place + step) % 4
            remote(
                near_ref.at[tile, :, pl.ds(pl.multiple_of(goal * 64, 64), 64)],
                far_ref.at[tile, place],
                send2.at[tile],
                recv2.at[tile],
                core,
                chip + (goal - place) * stride,
            ).start()
        pltpu.make_async_copy(
            near_ref.at[tile, :, pl.ds(pl.multiple_of(place * 64, 64), 64)],
            far_ref.at[tile, place],
            recv2.at[tile],
        ).start()

    cell = lax.broadcasted_iota(jnp.int32, (CELLS, 512), 0)
    for tile in range(TILES):
        drain(far_ref.at[tile], recv2.at[tile])
        for goal in range(4):
            slab = far_ref[tile, :, :, goal * CAP : (goal + 1) * CAP, :].reshape(512, 128)
            if tile < 3:
                ids = slab.T[127:128, :].astype(jnp.int32)
                hot_ref[tile, goal] = jnp.where(cell == ids, 1.0, 0.0).astype(jnp.bfloat16)
            member = hot_ref[tile % 3, goal]
            first = slab.astype(jnp.bfloat16)
            second = (slab - first.astype(jnp.float32)).astype(jnp.bfloat16)
            dense_ref[tile, goal] = jnp.dot(
                member, first, preferred_element_type=jnp.float32
            ) + jnp.dot(member, second, preferred_element_type=jnp.float32)
        place, stride = axis_of(tile, 2)
        for step in range(1, 4):
            goal = (place + step) % 4
            remote(
                dense_ref.at[tile, goal],
                last_ref.at[tile, place],
                send3.at[tile],
                recv3.at[tile],
                core,
                chip + (goal - place) * stride,
            ).start()
        pltpu.make_async_copy(
            dense_ref.at[tile, place], last_ref.at[tile, place], recv3.at[tile]
        ).start()
    for tile in range(TILES):
        drain(last_ref.at[tile], recv3.at[tile])
        own_ref[tile] = (
            last_ref[tile, 0] + last_ref[tile, 1] + last_ref[tile, 2] + last_ref[tile, 3]
        )

    swap = remote(own_ref, other_ref, send4.at[0], recv4.at[0], 1 - core, chip)
    swap.start()
    right = remote(
        own_ref.at[:, pl.ds(120, 8)], edge_ref.at[core], send4.at[1], recv4.at[1 + core], 0, after
    )
    right.start()
    left = remote(
        own_ref.at[:, pl.ds(0, 8)], edge_ref.at[core], send4.at[2], recv4.at[1 + core], 1, before
    )
    left.start()
    swap.wait()
    for row in range(2):
        drain(edge_ref.at[row], recv4.at[1 + row])
    right.wait_send()
    left.wait_send()

    def quads(tiles):
        full = jnp.concatenate([part[:, :WIDE] for part in tiles], axis=1)
        gap = jnp.zeros((full.shape[0], KP - KQ), jnp.float32)
        return [
            jnp.concatenate([full[:, q * KQ : (q + 1) * KQ], gap], axis=1) for q in range(4)
        ]

    for row in range(2):
        tiles = []
        sides = []
        for tile in range(TILES):
            own, other = own_ref[tile, mine, :], other_ref[tile, mine, :]
            columns = jnp.where(core == row, own, other)
            low = jnp.where(core == row, own_ref[tile, 56:72, :], other_ref[tile, 56:72, :])
            edge = edge_ref[row, tile] * inside
            rights = jnp.where(core == 0, low[8:9], edge[0:1])
            lefts = jnp.where(core == 0, edge[7:8], low[7:8])
            tiles.append(jnp.concatenate([columns, rights, gap, lefts], axis=0))
            sides.append(
                jnp.where(core == row, own_ref[tile, 128:136, :], other_ref[tile, 128:136, :])
            )
        for quad, value in enumerate(quads(tiles)):
            rim_ref[quad, row] = value
        for quad, value in enumerate(quads(sides)):
            for index in range(8):
                side_ref[quad, row * 8 + index] = value[index : index + 1]

    for tile in range(TILES):
        drain(near_ref.at[tile, pl.ds(0, 7)], send1.at[tile])
        drain(far_ref.at[tile, pl.ds(0, 3)], send2.at[tile])
        drain(last_ref.at[tile, pl.ds(0, 3)], send3.at[tile])


def exchange(source, points, ids, wind_speed, wind_dir, depth_class):
    dma = pltpu.SemaphoreType.DMA
    vmem = pl.BlockSpec(memory_space=pltpu.VMEM)
    count = points.shape[0]
    return pl.pallas_call(
        exchange_kernel,
        out_shape=(
            jax.ShapeDtypeStruct((4, 2, CW, KP), jnp.float32),
            jax.ShapeDtypeStruct((4, ROWS, 1, KP), jnp.float32),
            jax.ShapeDtypeStruct((CW, 128), jnp.float32),
        ),
        in_specs=[
            pl.BlockSpec(memory_space=pltpu.SMEM),
            pl.BlockSpec(memory_space=pl.ANY),
            vmem,
            vmem,
            vmem,
            vmem,
        ],
        out_specs=(vmem, vmem, vmem),
        scratch_shapes=[
            pltpu.VMEM(points.shape, jnp.float32),
            pltpu.VMEM((TILES, count + 8, 128), jnp.float32),
            pltpu.VMEM((2, TILES, 1024, 128), jnp.float32),
            pltpu.VMEM((TILES, 8, 256, 128), jnp.float32),
            pltpu.VMEM((TILES, 4, 8, 64, 128), jnp.float32),
            pltpu.VMEM((3, 4, CELLS, 512), jnp.bfloat16),
            pltpu.VMEM((TILES, 4, CELLS, 128), jnp.float32),
            pltpu.VMEM((TILES, 4, CELLS, 128), jnp.float32),
            pltpu.VMEM((TILES, CELLS, 128), jnp.float32),
            pltpu.VMEM((TILES, CELLS, 128), jnp.float32),
            pltpu.VMEM((2, TILES, 8, 128), jnp.float32),
            pltpu.VMEM((24, 128), jnp.float32),
            pltpu.VMEM((24, 128), jnp.float32),
            pltpu.VMEM((2, 24, 128), jnp.float32),
            pltpu.VMEM((128, 128), jnp.float32),
            dma((4,)),
            dma((TILES,)),
            dma((TILES,)),
            dma((TILES,)),
            dma((TILES,)),
            dma((TILES,)),
            dma((TILES,)),
            dma((3,)),
            dma((3,)),
            dma((3,)),
            dma((3,)),
        ],
        compiler_params=pltpu.CompilerParams(
            vmem_limit_bytes=52 << 20, collective_id=0, has_side_effects=True
        ),
        name="exchange_points",
    )(source, points, ids, wind_speed, wind_dir, depth_class)


def slot_sources(dest_cell, rows_dev, cols_dev):
    row_count = lax.axis_size("rows")
    col_count = lax.axis_size("cols")
    devices = row_count * col_count
    total_cols = cols_dev * col_count
    total_rows = rows_dev * row_count
    grid_row = dest_cell // total_cols
    grid_col = dest_cell % total_cols
    owner = grid_row // rows_dev * col_count + grid_col // cols_dev
    on_row = (grid_row == 0) | (grid_row == total_rows - 1)
    rim = jnp.where(on_row, grid_col % cols_dev, cols_dev + grid_row % rows_dev)
    position = jnp.arange(dest_cell.shape[0], dtype=jnp.int32)
    hot = owner[:, None] == jnp.arange(devices, dtype=jnp.int32)[None]
    before = (position[:, None] > position[None, :]).astype(jnp.bfloat16)
    earlier = jnp.dot(before, hot.astype(jnp.bfloat16), preferred_element_type=jnp.float32)
    rank = jnp.sum(jnp.where(hot, earlier, 0.0), axis=1).astype(jnp.int32)
    in_slot = rank[:, None] == jnp.arange(CAP, dtype=jnp.int32)[None]
    number = jnp.where(in_slot, (position + 1).astype(jnp.float32)[:, None], 0.0)
    source = lax.dot_general(
        hot.astype(jnp.float32),
        number,
        (((0,), (0,)), ((), ())),
        precision=lax.Precision.HIGHEST,
        preferred_element_type=jnp.float32,
    )
    source = source.astype(jnp.int32).reshape(-1)
    source = jnp.where(source > 0, source - 1, dest_cell.shape[0])
    return source, rim.astype(jnp.float32)[:, None]


def sweep_kernel(
    order_ref,
    cols_ref,
    rim_ref,
    side_ref,
    mask_ref,
    angle_ref,
    group_ref,
    rate_ref,
    matrix_ref,
    out_ref,
    wind_ref,
    speed_ref,
    loss_ref,
    trig_ref,
    high_ref,
    low_ref,
    state_ref,
    part_ref,
    total_ref,
    turned_ref,
    sem,
):
    total_ref[...] = jnp.zeros_like(total_ref)
    part_ref[...] = jnp.zeros_like(part_ref)
    trig_ref[...] = jnp.abs(angle_ref[...])

    tables = jnp.concatenate([group_ref[...], rate_ref[...]], axis=0)
    tables = jnp.concatenate(
        [tables] * QUARTER + [jnp.ones((tables.shape[0], KP - KQ), jnp.float32)], axis=1
    )
    rate = tables[8:9]
    edge = jnp.zeros((KQ, KP - KQ), jnp.float32)
    foot = jnp.zeros((KP - KQ, KP), jnp.float32)
    for quad in range(4):
        full = jnp.concatenate(
            [jnp.concatenate([matrix_ref[quad], edge], axis=1), foot], axis=0
        ).T
        rounded = full.astype(jnp.bfloat16)
        high_ref[quad] = rounded
        low_ref[quad] = (full - rounded.astype(jnp.float32)).astype(jnp.bfloat16)

    cols = cols_ref[...]
    cols_cos, cols_sin, cols_wind = jnp.cos(cols), jnp.sin(cols), (cols * 0.1) ** 2
    for row in range(ROWS):
        base = row // 8 * 24 + row % 8
        strength = rate * cols_wind[:, base : base + 1]
        toward = cols_cos[:, base + 8 : base + 9]
        aside = cols_sin[:, base + 8 : base + 9]
        kind = jnp.broadcast_to(cols[:, base + 16 : base + 17], (CW, KP))
        speed, loss = tables[0:1], tables[4:5]
        for index in range(1, 4):
            speed = jnp.where(kind == index, tables[index : index + 1], speed)
            loss = jnp.where(kind == index, tables[4 + index : 5 + index], loss)
        speed_ref[row] = speed
        loss_ref[row] = loss
        for quad in range(4):
            spread = jnp.maximum(
                angle_ref[quad, 0:1] * toward + angle_ref[quad, 1:2] * aside, 0.0
            )
            wind_ref[quad, row] = strength * (spread * spread)

    def wide(x):
        return jnp.concatenate([x, x], axis=1)

    def one_sweep(iteration, turn):
        quad = order_ref[iteration, turn]
        up_x = (quad == 0) | (quad == 3)
        up_y = quad < 2
        cos_row = trig_ref[quad, 0:1, :]
        sin_row = trig_ref[quad, 1:2, :]
        both = cos_row + sin_row

        def row_of(s):
            return jnp.where(up_x, s, ROWS - 1 - s)

        def factors(s):
            row = row_of(s)
            speed = speed_ref[row]
            energy = total_ref[row] * (1.0 / K)
            damp = whitecap_rate * energy / (1.0 + energy)
            den = both * speed + loss_ref[row] + wide(damp)
            inv = 1.0 / den
            known = wind_ref[quad, row] + mask_ref[...] * side_ref[quad, row]
            if s == 0 or s == ROWS - 1:
                known = known + rim_ref[quad, jnp.where(row == 0, 0, 1)]
            if iteration > 0:
                old = state_ref[quad, row]
                beside = jnp.where(up_y, pltpu.roll(old, 1, 0), pltpu.roll(old, CW - 1, 0))
                known = known + sin_row * speed * beside
            return (cos_row * speed) * inv, known * inv

        copies = []
        nxt = factors(0)
        upwind = None
        for s in range(ROWS):
            along, fixed = nxt
            balance = fixed if s == 0 else along * upwind + fixed
            first = balance.astype(jnp.bfloat16)
            second = (balance - first.astype(jnp.float32)).astype(jnp.bfloat16)
            high = high_ref[quad]
            new = (
                jnp.dot(first, high, preferred_element_type=jnp.float32)
                + jnp.dot(second, high, preferred_element_type=jnp.float32)
                + jnp.dot(first, low_ref[quad], preferred_element_type=jnp.float32)
            )
            if s + 1 < ROWS:
                nxt = factors(s + 1)
            row = row_of(s)
            if iteration == 0:
                state_ref[quad, row] = new
            square = jnp.sum(new * new, axis=1, keepdims=True)
            square = jnp.broadcast_to(square, (CW, 128))
            total = (
                part_ref[(quad + 1) % 4, row]
                + part_ref[(quad + 2) % 4, row]
                + part_ref[(quad + 3) % 4, row]
                + square
            )
            part_ref[quad, row] = square
            total_ref[row] = total
            if iteration == ITERS - 1:
                own = new[:HALF]
                turned_ref[s] = jnp.concatenate([own, own], axis=0).T[:KQ]
                copy = pltpu.make_async_copy(
                    turned_ref.at[s],
                    out_ref.at[pl.ds(quad * KQ, KQ), row],
                    sem.at[s],
                )
                copy.start()
                copies.append(copy)
            upwind = new
        for copy in copies:
            copy.wait()

    for iteration in range(ITERS):

        def turn_body(turn, carry, iteration=iteration):
            one_sweep(iteration, turn)
            return carry

        lax.fori_loop(0, 4, turn_body, 0)


def run_sweeps(order, cols, rim, side, mask, angles, groups, rate, matrix):
    vmem = pl.BlockSpec(memory_space=pltpu.VMEM)
    return pl.pallas_call(
        sweep_kernel,
        out_shape=jax.ShapeDtypeStruct((K, ROWS, 128), jnp.float32),
        in_specs=[pl.BlockSpec(memory_space=pltpu.SMEM)] + [vmem] * 8,
        out_specs=pl.BlockSpec(memory_space=pl.ANY),
        scratch_shapes=[
            pltpu.VMEM((4, ROWS, CW, KP), jnp.float32),
            pltpu.VMEM((ROWS, CW, KP), jnp.float32),
            pltpu.VMEM((ROWS, CW, KP), jnp.float32),
            pltpu.VMEM((4, 2, KP), jnp.float32),
            pltpu.VMEM((4, KP, KP), jnp.bfloat16),
            pltpu.VMEM((4, KP, KP), jnp.bfloat16),
            pltpu.VMEM((4, ROWS, CW, KP), jnp.float32),
            pltpu.VMEM((4, ROWS, CW, 128), jnp.float32),
            pltpu.VMEM((ROWS, CW, 128), jnp.float32),
            pltpu.VMEM((ROWS, KQ, 128), jnp.float32),
            pltpu.SemaphoreType.DMA((ROWS,)),
        ],
        compiler_params=pltpu.CompilerParams(vmem_limit_bytes=48 << 20),
        name="eight_sweeps",
    )(order, cols, rim, side, mask, angles, groups, rate, matrix)


def body(
    wind_speed,
    wind_dir,
    depth_class,
    group_speed,
    dissipation,
    input_rate,
    outer_spectra,
    dest_cell,
    refraction_inverse,
    sweep_order,
):
    rows_dev, cols_dev = wind_speed.shape
    col_count = lax.axis_size("cols")
    core = lax.axis_index("rows")
    chip = lax.axis_index("cols")
    swap = [(0, 1), (1, 0)]
    source, ids = slot_sources(dest_cell, rows_dev, cols_dev)
    rim_rows, side_rows, cols = exchange(
        source, outer_spectra, ids, wind_speed, wind_dir, depth_class
    )
    angle = (np.arange(NDIR, dtype=np.float64) + 0.5) * (2.0 * math.pi / NDIR)
    angle_k = np.repeat(angle, NFREQ).reshape(4, 1, KQ)
    angles = np.concatenate([np.cos(angle_k), np.sin(angle_k)], axis=1)
    angles = np.pad(angles, ((0, 0), (0, 0), (0, KP - KQ))).astype(np.float32)
    groups = jnp.concatenate([group_speed, dissipation], axis=0)
    at_col = jnp.where(
        (chip == 0) & (core == 0),
        0,
        jnp.where((chip == col_count - 1) & (core == 1), HALF - 1, CW),
    )
    mask = (jnp.arange(CW, dtype=jnp.int32) == at_col).astype(jnp.float32)
    mask = jnp.broadcast_to(mask[:, None], (CW, KP))

    out = run_sweeps(
        sweep_order,
        cols,
        rim_rows,
        side_rows,
        mask,
        jnp.asarray(angles),
        groups,
        input_rate[None],
        refraction_inverse,
    )
    keep = lax.dynamic_slice_in_dim(out, core * rows_dev, rows_dev, 1)
    give = lax.dynamic_slice_in_dim(out, (1 - core) * rows_dev, rows_dev, 1)
    taken = lax.ppermute(give, "rows", swap)
    lane_core = jnp.arange(cols_dev, dtype=jnp.int32) // HALF
    return jnp.where(lane_core == core, keep, taken)


def solution(mesh):
    placed = (
        P("rows", "cols"),
        P("rows", "cols"),
        P("rows", "cols"),
        P(),
        P(),
        P(),
        P(("rows", "cols"), None),
        P(("rows", "cols")),
        P(),
        P(),
    )
    return jax.shard_map(
        body, mesh=mesh, in_specs=placed, out_specs=P(None, "rows", "cols"), check_vma=False
    )
```

```python
import math

import jax
import jax.numpy as jnp
import numpy as np
from jax import lax
from jax.experimental import pallas as pl
from jax.experimental.pallas import tpu as pltpu
from jax.sharding import PartitionSpec as P

NDIR = 36
NFREQ = 24
CAP = 16
ITERS = 2
QUARTER = NDIR // 4
KQ = QUARTER * NFREQ
KP = 256
K = 4 * KQ
TILES = 7
WIDE = 124
CELLS = 144
ROWS = 16
HALF = 64
CW = 72

whitecap_rate = 0.5


def place_of(order, dest):
    at = (dest % 4, dest // 4 % 4, dest // 16)
    return at[order] * 16 + at[(order + 1) % 3] * 4 + at[(order + 2) % 3]


def exchange_kernel(
    source_ref,
    points_ref,
    id_ref,
    speed_ref,
    dir_ref,
    class_ref,
    rim_ref,
    side_ref,
    cols_ref,
    load_ref,
    stage_ref,
    slots_ref,
    near_ref,
    far_ref,
    hot_ref,
    dense_ref,
    last_ref,
    own_ref,
    other_ref,
    edge_ref,
    field_ref,
    field_other_ref,
    field_edge_ref,
    turn_ref,
    load_sem,
    send1,
    recv1,
    send2,
    recv2,
    send3,
    recv3,
    send4,
    recv4,
    send5,
    recv5,
):
    core = lax.axis_index("rows")
    chip = lax.axis_index("cols")
    strides = (1, 4, 16)
    at = tuple(chip // stride % 4 for stride in strides)
    chips = 64

    def moved(axis, value):
        return chip + (value - at[axis]) * strides[axis]

    def remote(src, dst, send, recv, row, col):
        return pltpu.make_async_remote_copy(
            src_ref=src,
            dst_ref=dst,
            send_sem=send,
            recv_sem=recv,
            device_id=(row, col),
            device_id_type=pl.DeviceIdType.MESH,
        )

    def drain(ref, sem):
        pltpu.make_async_copy(ref, ref, sem).wait()

    count = points_ref.shape[1]
    loads = []
    for step in range(4):
        rows = pl.ds(step * KQ, KQ)
        load = pltpu.make_async_copy(points_ref.at[rows], load_ref.at[rows], load_sem.at[step])
        load.start()
        loads.append(load)
    field_ref[0:8] = speed_ref[...]
    field_ref[8:16] = dir_ref[...]
    field_ref[16:24] = class_ref[...].astype(jnp.float32)

    barrier = pltpu.get_barrier_semaphore()

    def greet(row, col):
        pl.semaphore_signal(
            barrier, inc=1, device_id=(row, col), device_id_type=pl.DeviceIdType.MESH
        )

    for axis in range(3):
        for step in range(1, 4):
            for row in range(2):
                greet(row, moved(axis, (at[axis] + step) % 4))
    greet(1 - core, chip)

    after, before = (chip + 1) % chips, (chip + chips - 1) % chips
    greet(0, after)
    greet(1, before)
    greet(core, (chip + chips - 1 + 2 * core) % chips)
    pl.semaphore_wait(barrier, 22)

    trades = []
    for index, (row, col) in enumerate(((1 - core, chip), (0, after), (1, before))):
        goal_ref = field_other_ref if index == 0 else field_edge_ref.at[core]
        arrival = recv5.at[0] if index == 0 else recv5.at[1 + core]
        trade = remote(field_ref, goal_ref, send5.at[index], arrival, row, col)
        trade.start()
        trades.append(trade)

    sublane = lax.broadcasted_iota(jnp.int32, (8, 128), 0)
    load_ref[K:] = jnp.zeros((load_ref.shape[0] - K, count), jnp.float32)
    ids = jnp.broadcast_to(id_ref[...], (128 - WIDE, count))
    for group in ((0,), (1, 2), (3, 4), (5, 6)):
        if group[0] < 2:
            for load in loads[:1] if group[0] == 0 else loads[1:]:
                load.wait()
        for tile in group:
            block = load_ref[tile * WIDE : (tile + 1) * WIDE]
            stage_ref[tile, 0:count] = jnp.concatenate([block, ids], axis=0).T
            stage_ref[tile, count:] = jnp.zeros((8, 128), jnp.float32)
        for row in range(2):

            def place(dest, carry, row=row, group=group):
                starts = [place_of((tile + row) % 3, dest) * CAP for tile in group]
                for half in range(2):
                    tiles = [None] * len(group)
                    for lane in range(8):
                        point = source_ref[row * 1024 + dest * CAP + half * 8 + lane]
                        for index, tile in enumerate(group):
                            found = stage_ref.at[tile][pl.ds(point, 8, stride=0), :]
                            tiles[index] = (
                                found
                                if lane == 0
                                else jnp.where(sublane == lane, found, tiles[index])
                            )
                    for index, tile in enumerate(group):
                        start = pl.multiple_of(starts[index] + half * 8, 8)
                        slots_ref[row, tile, pl.ds(start, 8), :] = tiles[index]
                return carry

            lax.fori_loop(0, 64, place, 0)
        for tile in group:
            for row in range(2):
                axis = (tile + row) % 3
                mine = core * 4 + at[axis]
                for step in range(1, 4):
                    goal = (at[axis] + step) % 4
                    remote(
                        slots_ref.at[row, tile, pl.ds(pl.multiple_of(goal * 256, 256), 256)],
                        near_ref.at[tile, mine],
                        send1.at[tile],
                        recv1.at[tile],
                        row,
                        moved(axis, goal),
                    ).start()
                rest = slots_ref.at[row, tile, pl.ds(pl.multiple_of(at[axis] * 256, 256), 256)]

                @pl.when(core != row)
                def _():
                    remote(
                        rest, near_ref.at[tile, mine], send1.at[tile], recv1.at[tile], row, chip
                    ).start()

                @pl.when(core == row)
                def _():
                    pltpu.make_async_copy(rest, near_ref.at[tile, mine], recv1.at[tile]).start()

    outside = jnp.where(core == 0, chip == 0, chip == chips - 1)
    inside = jnp.where(outside, 0.0, 1.0)
    for trade in trades:
        trade.wait_send()
    drain(field_other_ref, recv5.at[0])
    for row in range(2):
        drain(field_edge_ref.at[row], recv5.at[1 + row])
    own_field, other_field = field_ref[...], field_other_ref[...]
    pad = jnp.zeros((80, 128), jnp.float32)
    both = [jnp.where(core == row, own_field, other_field) for row in range(2)]
    turn_ref[...] = jnp.concatenate(both + [pad], axis=0).T
    edges = jnp.concatenate([field_edge_ref[0], field_edge_ref[1], pad], axis=0).T * inside
    middle = turn_ref[56:72]
    mine = pl.ds(pl.multiple_of(core * HALF, HALF), HALF)
    gap = jnp.zeros((6, 128), jnp.float32)
    cols_ref[...] = jnp.concatenate(
        [
            turn_ref[mine],
            jnp.where(core == 0, middle[8:9], edges[0:1]),
            gap,
            jnp.where(core == 0, edges[127:128], middle[7:8]),
        ],
        axis=0,
    )

    def axis_of(tile, turn):
        even = (tile + turn) % 3
        odd = (tile + 1 + turn) % 3
        place = (1 - core) * at[even] + core * at[odd]
        stride = (1 - core) * strides[even] + core * strides[odd]
        return place, stride

    for tile in range(TILES):
        drain(near_ref.at[tile], recv1.at[tile])
        place, stride = axis_of(tile, 1)
        for step in range(1, 4):
            goal = (place + step) % 4
            remote(
                near_ref.at[tile, :, pl.ds(pl.multiple_of(goal * 64, 64), 64)],
                far_ref.at[tile, place],
                send2.at[tile],
                recv2.at[tile],
                core,
                chip + (goal - place) * stride,
            ).start()
        pltpu.make_async_copy(
            near_ref.at[tile, :, pl.ds(pl.multiple_of(place * 64, 64), 64)],
            far_ref.at[tile, place],
            recv2.at[tile],
        ).start()

    cell = lax.broadcasted_iota(jnp.int32, (CELLS, 512), 0)
    for tile in range(TILES):
        drain(far_ref.at[tile], recv2.at[tile])
        for goal in range(4):
            slab = far_ref[tile, :, :, goal * CAP : (goal + 1) * CAP, :].reshape(512, 128)
            if tile < 3:
                ids = slab.T[127:128, :].astype(jnp.int32)
                hot_ref[tile, goal] = jnp.where(cell == ids, 1.0, 0.0).astype(jnp.bfloat16)
            member = hot_ref[tile % 3, goal]
            first = slab.astype(jnp.bfloat16)
            second = (slab - first.astype(jnp.float32)).astype(jnp.bfloat16)
            dense_ref[tile, goal] = jnp.dot(
                member, first, preferred_element_type=jnp.float32
            ) + jnp.dot(member, second, preferred_element_type=jnp.float32)
        place, stride = axis_of(tile, 2)
        for step in range(1, 4):
            goal = (place + step) % 4
            remote(
                dense_ref.at[tile, goal],
                last_ref.at[tile, place],
                send3.at[tile],
                recv3.at[tile],
                core,
                chip + (goal - place) * stride,
            ).start()
        pltpu.make_async_copy(
            dense_ref.at[tile, place], last_ref.at[tile, place], recv3.at[tile]
        ).start()
    for tile in range(TILES):
        drain(last_ref.at[tile], recv3.at[tile])
        own_ref[tile] = (
            last_ref[tile, 0] + last_ref[tile, 1] + last_ref[tile, 2] + last_ref[tile, 3]
        )

    swap = remote(own_ref, other_ref, send4.at[0], recv4.at[0], 1 - core, chip)
    swap.start()
    right = remote(
        own_ref.at[:, pl.ds(120, 8)], edge_ref.at[core], send4.at[1], recv4.at[1 + core], 0, after
    )
    right.start()
    left = remote(
        own_ref.at[:, pl.ds(0, 8)], edge_ref.at[core], send4.at[2], recv4.at[1 + core], 1, before
    )
    left.start()
    swap.wait()
    for row in range(2):
        drain(edge_ref.at[row], recv4.at[1 + row])
    right.wait_send()
    left.wait_send()

    def quads(tiles):
        full = jnp.concatenate([part[:, :WIDE] for part in tiles], axis=1)
        gap = jnp.zeros((full.shape[0], KP - KQ), jnp.float32)
        return [
            jnp.concatenate([full[:, q * KQ : (q + 1) * KQ], gap], axis=1) for q in range(4)
        ]

    for row in range(2):
        tiles = []
        sides = []
        for tile in range(TILES):
            own, other = own_ref[tile, mine, :], other_ref[tile, mine, :]
            columns = jnp.where(core == row, own, other)
            low = jnp.where(core == row, own_ref[tile, 56:72, :], other_ref[tile, 56:72, :])
            edge = edge_ref[row, tile] * inside
            rights = jnp.where(core == 0, low[8:9], edge[0:1])
            lefts = jnp.where(core == 0, edge[7:8], low[7:8])
            tiles.append(jnp.concatenate([columns, rights, gap, lefts], axis=0))
            sides.append(
                jnp.where(core == row, own_ref[tile, 128:136, :], other_ref[tile, 128:136, :])
            )
        for quad, value in enumerate(quads(tiles)):
            rim_ref[quad, row] = value
        for quad, value in enumerate(quads(sides)):
            for index in range(8):
                side_ref[quad, row * 8 + index] = value[index : index + 1]

    for tile in range(TILES):
        drain(near_ref.at[tile, pl.ds(0, 7)], send1.at[tile])
        drain(far_ref.at[tile, pl.ds(0, 3)], send2.at[tile])
        drain(last_ref.at[tile, pl.ds(0, 3)], send3.at[tile])


def exchange(source, points, ids, wind_speed, wind_dir, depth_class):
    dma = pltpu.SemaphoreType.DMA
    vmem = pl.BlockSpec(memory_space=pltpu.VMEM)
    count = points.shape[1]
    return pl.pallas_call(
        exchange_kernel,
        out_shape=(
            jax.ShapeDtypeStruct((4, 2, CW, KP), jnp.float32),
            jax.ShapeDtypeStruct((4, ROWS, 1, KP), jnp.float32),
            jax.ShapeDtypeStruct((CW, 128), jnp.float32),
        ),
        in_specs=[
            pl.BlockSpec(memory_space=pltpu.SMEM),
            pl.BlockSpec(memory_space=pl.ANY),
            vmem,
            vmem,
            vmem,
            vmem,
        ],
        out_specs=(vmem, vmem, vmem),
        scratch_shapes=[
            pltpu.VMEM((K + 8, count), jnp.float32),
            pltpu.VMEM((TILES, count + 8, 128), jnp.float32),
            pltpu.VMEM((2, TILES, 1024, 128), jnp.float32),
            pltpu.VMEM((TILES, 8, 256, 128), jnp.float32),
            pltpu.VMEM((TILES, 4, 8, 64, 128), jnp.float32),
            pltpu.VMEM((3, 4, CELLS, 512), jnp.bfloat16),
            pltpu.VMEM((TILES, 4, CELLS, 128), jnp.float32),
            pltpu.VMEM((TILES, 4, CELLS, 128), jnp.float32),
            pltpu.VMEM((TILES, CELLS, 128), jnp.float32),
            pltpu.VMEM((TILES, CELLS, 128), jnp.float32),
            pltpu.VMEM((2, TILES, 8, 128), jnp.float32),
            pltpu.VMEM((24, 128), jnp.float32),
            pltpu.VMEM((24, 128), jnp.float32),
            pltpu.VMEM((2, 24, 128), jnp.float32),
            pltpu.VMEM((128, 128), jnp.float32),
            dma((4,)),
            dma((TILES,)),
            dma((TILES,)),
            dma((TILES,)),
            dma((TILES,)),
            dma((TILES,)),
            dma((TILES,)),
            dma((3,)),
            dma((3,)),
            dma((3,)),
            dma((3,)),
        ],
        compiler_params=pltpu.CompilerParams(
            vmem_limit_bytes=52 << 20, collective_id=0, has_side_effects=True
        ),
        name="exchange_points",
    )(source, points, ids, wind_speed, wind_dir, depth_class)


def slot_sources(dest_cell, rows_dev, cols_dev):
    row_count = lax.axis_size("rows")
    col_count = lax.axis_size("cols")
    devices = row_count * col_count
    total_cols = cols_dev * col_count
    total_rows = rows_dev * row_count
    grid_row = dest_cell // total_cols
    grid_col = dest_cell % total_cols
    owner = grid_row // rows_dev * col_count + grid_col // cols_dev
    on_row = (grid_row == 0) | (grid_row == total_rows - 1)
    rim = jnp.where(on_row, grid_col % cols_dev, cols_dev + grid_row % rows_dev)
    position = jnp.arange(dest_cell.shape[0], dtype=jnp.int32)
    hot = owner[:, None] == jnp.arange(devices, dtype=jnp.int32)[None]
    before = (position[:, None] > position[None, :]).astype(jnp.bfloat16)
    earlier = jnp.dot(before, hot.astype(jnp.bfloat16), preferred_element_type=jnp.float32)
    rank = jnp.sum(jnp.where(hot, earlier, 0.0), axis=1).astype(jnp.int32)
    in_slot = rank[:, None] == jnp.arange(CAP, dtype=jnp.int32)[None]
    number = jnp.where(in_slot, (position + 1).astype(jnp.float32)[:, None], 0.0)
    source = lax.dot_general(
        hot.astype(jnp.float32),
        number,
        (((0,), (0,)), ((), ())),
        precision=lax.Precision.HIGHEST,
        preferred_element_type=jnp.float32,
    )
    source = source.astype(jnp.int32).reshape(-1)
    source = jnp.where(source > 0, source - 1, dest_cell.shape[0])
    return source, rim.astype(jnp.float32)[None]


def sweep_kernel(
    order_ref,
    cols_ref,
    rim_ref,
    side_ref,
    mask_ref,
    angle_ref,
    group_ref,
    rate_ref,
    matrix_ref,
    keep_ref,
    give_ref,
    wind_ref,
    speed_ref,
    loss_ref,
    trig_ref,
    high_ref,
    low_ref,
    state_ref,
    part_ref,
    damp_ref,
    damp_next_ref,
    final_ref,
    turned_ref,
    sem,
):
    damp_ref[...] = jnp.zeros_like(damp_ref)
    part_ref[...] = jnp.zeros_like(part_ref)
    trig_ref[...] = jnp.abs(angle_ref[...])

    tables = jnp.concatenate([group_ref[...], rate_ref[...]], axis=0)
    tables = jnp.concatenate(
        [tables] * QUARTER + [jnp.ones((tables.shape[0], KP - KQ), jnp.float32)], axis=1
    )
    rate = tables[8:9]
    edge = jnp.zeros((KQ, KP - KQ), jnp.float32)
    foot = jnp.zeros((KP - KQ, KP), jnp.float32)
    for quad in range(4):
        full = jnp.concatenate(
            [jnp.concatenate([matrix_ref[quad], edge], axis=1), foot], axis=0
        ).T
        rounded = full.astype(jnp.bfloat16)
        high_ref[quad] = rounded
        low_ref[quad] = (full - rounded.astype(jnp.float32)).astype(jnp.bfloat16)

    cols = cols_ref[...]
    cols_cos, cols_sin, cols_wind = jnp.cos(cols), jnp.sin(cols), (cols * 0.1) ** 2
    for row in range(ROWS):
        base = row // 8 * 24 + row % 8
        strength = rate * cols_wind[:, base : base + 1]
        toward = cols_cos[:, base + 8 : base + 9]
        aside = cols_sin[:, base + 8 : base + 9]
        kind = jnp.broadcast_to(cols[:, base + 16 : base + 17], (CW, KP))
        speed, loss = tables[0:1], tables[4:5]
        for index in range(1, 4):
            speed = jnp.where(kind == index, tables[index : index + 1], speed)
            loss = jnp.where(kind == index, tables[4 + index : 5 + index], loss)
        speed_ref[row] = speed
        loss_ref[row] = loss
        for quad in range(4):
            spread = jnp.maximum(
                angle_ref[quad, 0:1] * toward + angle_ref[quad, 1:2] * aside, 0.0
            )
            source = strength * (spread * spread) + mask_ref[...] * side_ref[quad, row]
            if row == 0:
                source = source + rim_ref[quad, 0]
            elif row == ROWS - 1:
                source = source + rim_ref[quad, 1]
            wind_ref[quad, row] = source

    def wide(x):
        return jnp.concatenate([x, x], axis=1)

    core = lax.axis_index("rows")

    def one_sweep(iteration, turn, turn_half, damp_from, damp_to):
        quad = order_ref[iteration, turn]
        up_x = (quad == 0) | (quad == 3)
        up_y = quad < 2
        cos_row = trig_ref[quad, 0:1, :]
        sin_row = trig_ref[quad, 1:2, :]
        both = cos_row + sin_row

        def row_of(s):
            return jnp.where(up_x, s, ROWS - 1 - s)

        def factors(s):
            row = row_of(s)
            speed = speed_ref[row]
            den = both * speed + loss_ref[row] + wide(damp_from[row])
            inv = 1.0 / den
            known = wind_ref[quad, row]
            if iteration > 0:
                old = state_ref[quad, row]
                beside = jnp.where(up_y, pltpu.roll(old, 1, 0), pltpu.roll(old, CW - 1, 0))
                known = known + sin_row * speed * beside
            return (cos_row * speed) * inv, known * inv

        copies = []
        nxt = factors(0)
        upwind = None
        for s in range(ROWS):
            along, fixed = nxt
            balance = fixed if s == 0 else along * upwind + fixed
            first = balance.astype(jnp.bfloat16)
            second = (balance - first.astype(jnp.float32)).astype(jnp.bfloat16)
            stacked = jnp.dot(jnp.concatenate([first, second], axis=0), high_ref[quad], preferred_element_type=jnp.float32)
            new = stacked[:CW] + stacked[CW:] + jnp.dot(first, low_ref[quad], preferred_element_type=jnp.float32)
            if s + 1 < ROWS:
                nxt = factors(s + 1)
            row = row_of(s)
            if iteration == 0:
                state_ref[quad, row] = new
            square = jnp.sum(new * new, axis=1, keepdims=True)
            square = jnp.broadcast_to(square, (CW, 128))
            total = (
                part_ref[(quad + 1) % 4, row]
                + part_ref[(quad + 2) % 4, row]
                + part_ref[(quad + 3) % 4, row]
                + square
            )
            part_ref[quad, row] = square
            energy = total * (1.0 / K)
            damp_to[row] = whitecap_rate * energy / (1.0 + energy)
            if iteration == ITERS - 1 and turn_half == 0:
                final_ref[row] = new[:HALF]
            if iteration == ITERS - 1 and turn_half == 1:
                turned_ref[s] = jnp.concatenate([final_ref[row], new[:HALF]], axis=0).T[:KQ]
                place = (pl.ds(turn // 2 * KQ, KQ), row % 8)

                @pl.when(row // 8 == core)
                def _():
                    pltpu.make_async_copy(
                        turned_ref.at[s], keep_ref.at[place], sem.at[s]
                    ).start()

                @pl.when(row // 8 != core)
                def _():
                    pltpu.make_async_copy(
                        turned_ref.at[s], give_ref.at[place], sem.at[s]
                    ).start()

                copies.append(
                    pltpu.make_async_copy(turned_ref.at[s], keep_ref.at[place], sem.at[s])
                )
            upwind = new
        for copy in copies:
            copy.wait()

    for iteration in range(ITERS):

        def two_turns(pair, carry, iteration=iteration):
            one_sweep(iteration, 2 * pair, 0, damp_ref, damp_next_ref)
            one_sweep(iteration, 2 * pair + 1, 1, damp_next_ref, damp_ref)
            return carry

        lax.fori_loop(0, 2, two_turns, 0)


def run_sweeps(order, cols, rim, side, mask, angles, groups, rate, matrix):
    vmem = pl.BlockSpec(memory_space=pltpu.VMEM)
    return pl.pallas_call(
        sweep_kernel,
        out_shape=(jax.ShapeDtypeStruct((2 * KQ, ROWS // 2, 128), jnp.float32),) * 2,
        in_specs=[pl.BlockSpec(memory_space=pltpu.SMEM)] + [vmem] * 8,
        out_specs=(pl.BlockSpec(memory_space=pl.ANY),) * 2,
        scratch_shapes=[
            pltpu.VMEM((4, ROWS, CW, KP), jnp.float32),
            pltpu.VMEM((ROWS, CW, KP), jnp.float32),
            pltpu.VMEM((ROWS, CW, KP), jnp.float32),
            pltpu.VMEM((4, 2, KP), jnp.float32),
            pltpu.VMEM((4, KP, KP), jnp.bfloat16),
            pltpu.VMEM((4, KP, KP), jnp.bfloat16),
            pltpu.VMEM((4, ROWS, CW, KP), jnp.float32),
            pltpu.VMEM((4, ROWS, CW, 128), jnp.float32),
            pltpu.VMEM((ROWS, CW, 128), jnp.float32),
            pltpu.VMEM((ROWS, CW, 128), jnp.float32),
            pltpu.VMEM((ROWS, HALF, KP), jnp.float32),
            pltpu.VMEM((ROWS, KQ, 128), jnp.float32),
            pltpu.SemaphoreType.DMA((ROWS,)),
        ],
        compiler_params=pltpu.CompilerParams(vmem_limit_bytes=48 << 20),
        name="eight_sweeps",
    )(order, cols, rim, side, mask, angles, groups, rate, matrix)


def join_kernel(order_ref, keep_ref, got_ref, out_ref):
    core = lax.axis_index("rows")
    half = pl.program_id(2)
    lane = lax.broadcasted_iota(jnp.int32, out_ref.shape, 2)
    mine = lane // HALF == core

    @pl.when(half == core)
    def _():
        out_ref[...] = jnp.where(mine, keep_ref[...], pltpu.roll(got_ref[...], HALF, 2))

    @pl.when(half != core)
    def _():
        out_ref[...] = jnp.where(mine, pltpu.roll(keep_ref[...], HALF, 2), got_ref[...])


def join(order, keep, got):
    parts = 3
    rows, lanes = keep.shape[1:]
    block = (KQ // parts, rows, lanes)

    def pair_of(pair, part, half, order_ref):
        return (pair * parts + part, 0, 0)

    def quad_of(pair, part, half, order_ref):
        return (order_ref[ITERS - 1, pair * 2 + half] * parts + part, 0, 0)

    return pl.pallas_call(
        join_kernel,
        out_shape=jax.ShapeDtypeStruct((K, rows, lanes), jnp.float32),
        grid_spec=pltpu.PrefetchScalarGridSpec(
            num_scalar_prefetch=1,
            grid=(2, parts, 2),
            in_specs=[pl.BlockSpec(block, pair_of), pl.BlockSpec(block, pair_of)],
            out_specs=pl.BlockSpec(block, quad_of),
        ),
        compiler_params=pltpu.CompilerParams(vmem_limit_bytes=24 << 20),
        name="join_cores",
    )(order, keep, got)


def body(
    wind_speed,
    wind_dir,
    depth_class,
    group_speed,
    dissipation,
    input_rate,
    outer_spectra,
    dest_cell,
    refraction_inverse,
    sweep_order,
):
    rows_dev, cols_dev = wind_speed.shape
    col_count = lax.axis_size("cols")
    core = lax.axis_index("rows")
    chip = lax.axis_index("cols")
    swap = [(0, 1), (1, 0)]
    source, ids = slot_sources(dest_cell, rows_dev, cols_dev)
    rim_rows, side_rows, cols = exchange(
        source, outer_spectra.T, ids, wind_speed, wind_dir, depth_class
    )
    angle = (np.arange(NDIR, dtype=np.float64) + 0.5) * (2.0 * math.pi / NDIR)
    angle_k = np.repeat(angle, NFREQ).reshape(4, 1, KQ)
    angles = np.concatenate([np.cos(angle_k), np.sin(angle_k)], axis=1)
    angles = np.pad(angles, ((0, 0), (0, 0), (0, KP - KQ))).astype(np.float32)
    groups = jnp.concatenate([group_speed, dissipation], axis=0)
    at_col = jnp.where(
        (chip == 0) & (core == 0),
        0,
        jnp.where((chip == col_count - 1) & (core == 1), HALF - 1, CW),
    )
    mask = (jnp.arange(CW, dtype=jnp.int32) == at_col).astype(jnp.float32)
    mask = jnp.broadcast_to(mask[:, None], (CW, KP))

    keep, give = run_sweeps(
        sweep_order,
        cols,
        rim_rows,
        side_rows,
        mask,
        jnp.asarray(angles),
        groups,
        input_rate[None],
        refraction_inverse,
    )
    return join(sweep_order, keep, lax.ppermute(give, "rows", swap))


def solution(mesh):
    placed = (
        P("rows", "cols"),
        P("rows", "cols"),
        P("rows", "cols"),
        P(),
        P(),
        P(),
        P(("rows", "cols"), None),
        P(("rows", "cols")),
        P(),
        P(),
    )
    return jax.shard_map(
        body, mesh=mesh, in_specs=placed, out_specs=P(None, "rows", "cols"), check_vma=False
    )
```

```python
import math

import jax
import jax.numpy as jnp
import numpy as np
from jax import lax
from jax.experimental import pallas as pl
from jax.experimental.pallas import tpu as pltpu
from jax.sharding import PartitionSpec as P

NDIR = 36
NFREQ = 24
CAP = 16
ITERS = 2
QUARTER = NDIR // 4
KQ = QUARTER * NFREQ
KP = 256
K = 4 * KQ
TILES = 7
WIDE = 124
CELLS = 144
ROWS = 16
HALF = 64
CW = 72

whitecap_rate = 0.5


def place_of(order, dest):
    at = (dest % 4, dest // 4 % 4, dest // 16)
    return at[order] * 16 + at[(order + 1) % 3] * 4 + at[(order + 2) % 3]


def wave_kernel(
    source_ref,
    order_ref,
    points_ref,
    id_ref,
    wind_speed_ref,
    wind_dir_ref,
    class_ref,
    angle_ref,
    group_ref,
    dissipation_ref,
    rate_ref,
    matrix_ref,
    keep_ref,
    got_ref,
    load_ref,
    stage_ref,
    slots_ref,
    near_ref,
    far_ref,
    hot_ref,
    dense_ref,
    last_ref,
    own_ref,
    other_ref,
    edge_ref,
    field_ref,
    field_other_ref,
    field_edge_ref,
    turn_ref,
    wind_ref,
    speed_ref,
    loss_ref,
    trig_ref,
    high_ref,
    low_ref,
    state_ref,
    part_ref,
    damp_ref,
    damp_next_ref,
    final_ref,
    turned_ref,
    leave_ref,
    load_sem,
    send1,
    recv1,
    send2,
    recv2,
    send3,
    recv3,
    send4,
    recv4,
    send_edge,
    recv_edge,
    send5,
    recv5,
    save_sem,
    send6,
    recv6,
):
    core = lax.axis_index("rows")
    chip = lax.axis_index("cols")
    strides = (1, 4, 16)
    at = tuple(chip // stride % 4 for stride in strides)
    chips = 64

    def moved(axis, value):
        return chip + (value - at[axis]) * strides[axis]

    def remote(src, dst, send, recv, row, col):
        return pltpu.make_async_remote_copy(
            src_ref=src,
            dst_ref=dst,
            send_sem=send,
            recv_sem=recv,
            device_id=(row, col),
            device_id_type=pl.DeviceIdType.MESH,
        )

    def drain(ref, sem):
        pltpu.make_async_copy(ref, ref, sem).wait()

    count = points_ref.shape[1]
    loads = []
    for step in range(4):
        rows = pl.ds(step * KQ, KQ)
        load = pltpu.make_async_copy(points_ref.at[rows], load_ref.at[step], load_sem.at[step])
        load.start()
        loads.append(load)
    field_ref[0:8] = wind_speed_ref[...]
    field_ref[8:16] = wind_dir_ref[...]
    field_ref[16:24] = class_ref[...].astype(jnp.float32)

    barrier = pltpu.get_barrier_semaphore()

    def greet(row, col):
        pl.semaphore_signal(
            barrier, inc=1, device_id=(row, col), device_id_type=pl.DeviceIdType.MESH
        )

    for axis in range(3):
        for step in range(1, 4):
            for row in range(2):
                greet(row, moved(axis, (at[axis] + step) % 4))
    greet(1 - core, chip)

    after, before = (chip + 1) % chips, (chip + chips - 1) % chips
    greet(0, after)
    greet(1, before)
    greet(core, (chip + chips - 1 + 2 * core) % chips)
    pl.semaphore_wait(barrier, 22)

    trades = []
    for index, (row, col) in enumerate(((1 - core, chip), (0, after), (1, before))):
        goal_ref = field_other_ref if index == 0 else field_edge_ref.at[core]
        arrival = recv5.at[0] if index == 0 else recv5.at[1 + core]
        trade = remote(field_ref, goal_ref, send5.at[index], arrival, row, col)
        trade.start()
        trades.append(trade)

    sublane = lax.broadcasted_iota(jnp.int32, (8, 128), 0)
    for load in loads:
        load.wait()
    ids = jnp.broadcast_to(id_ref[...], (128 - WIDE, count))
    for group in ((0,), (1, 2), (3, 4), (5, 6)):
        for tile in group:
            pieces, low = [], tile * WIDE
            while low < min(tile * WIDE + WIDE, K):
                turn = low // KQ
                high = min(tile * WIDE + WIDE, turn * KQ + KQ)
                pieces.append(load_ref[order_ref[0, turn], low - turn * KQ : high - turn * KQ, :])
                low = high
            if low < tile * WIDE + WIDE:
                pieces.append(jnp.zeros((tile * WIDE + WIDE - low, count), jnp.float32))
            stage_ref[tile % 2, 0:count] = jnp.concatenate(pieces + [ids], axis=0).T
            stage_ref[tile % 2, count:] = jnp.zeros((8, 128), jnp.float32)
        for row in range(2):

            def place(dest, carry, row=row, group=group):
                starts = [place_of((tile + row) % 3, dest) * CAP for tile in group]
                for half in range(2):
                    tiles = [None] * len(group)
                    for lane in range(8):
                        point = source_ref[row * 1024 + dest * CAP + half * 8 + lane]
                        for index, tile in enumerate(group):
                            found = stage_ref.at[tile % 2][pl.ds(point, 8, stride=0), :]
                            tiles[index] = (
                                found
                                if lane == 0
                                else jnp.where(sublane == lane, found, tiles[index])
                            )
                    for index, tile in enumerate(group):
                        start = pl.multiple_of(starts[index] + half * 8, 8)
                        slots_ref[row, tile, pl.ds(start, 8), :] = tiles[index]
                return carry

            lax.fori_loop(0, 64, place, 0)
        for tile in group:
            for row in range(2):
                axis = (tile + row) % 3
                mine = core * 4 + at[axis]
                for step in range(1, 4):
                    goal = (at[axis] + step) % 4
                    remote(
                        slots_ref.at[row, tile, pl.ds(pl.multiple_of(goal * 256, 256), 256)],
                        near_ref.at[tile, mine],
                        send1.at[tile],
                        recv1.at[tile],
                        row,
                        moved(axis, goal),
                    ).start()
                rest = slots_ref.at[row, tile, pl.ds(pl.multiple_of(at[axis] * 256, 256), 256)]

                @pl.when(core != row)
                def _():
                    remote(
                        rest, near_ref.at[tile, mine], send1.at[tile], recv1.at[tile], row, chip
                    ).start()

                @pl.when(core == row)
                def _():
                    pltpu.make_async_copy(rest, near_ref.at[tile, mine], recv1.at[tile]).start()

    outside = jnp.where(core == 0, chip == 0, chip == chips - 1)
    inside = jnp.where(outside, 0.0, 1.0)
    for trade in trades:
        trade.wait_send()
    drain(field_other_ref, recv5.at[0])
    for row in range(2):
        drain(field_edge_ref.at[row], recv5.at[1 + row])
    own_field, other_field = field_ref[...], field_other_ref[...]
    pad = jnp.zeros((80, 128), jnp.float32)
    both = [jnp.where(core == row, own_field, other_field) for row in range(2)]
    turn_ref[...] = jnp.concatenate(both + [pad], axis=0).T
    edges = jnp.concatenate([field_edge_ref[0], field_edge_ref[1], pad], axis=0).T * inside
    middle = turn_ref[56:72]
    mine = pl.ds(pl.multiple_of(core * HALF, HALF), HALF)
    gap = jnp.zeros((6, 128), jnp.float32)
    cols = jnp.concatenate(
        [
            turn_ref[mine],
            jnp.where(core == 0, middle[8:9], edges[0:1]),
            gap,
            jnp.where(core == 0, edges[127:128], middle[7:8]),
        ],
        axis=0,
    )

    cols_cos, cols_sin, cols_wind = jnp.cos(cols), jnp.sin(cols), (cols * 0.1) ** 2

    def over_quadrant(table):
        fill = jnp.ones((table.shape[0], KP - KQ), jnp.float32)
        return jnp.concatenate([table] * QUARTER + [fill], axis=1)

    groups = over_quadrant(group_ref[...])
    losses = over_quadrant(dissipation_ref[...])
    rate = over_quadrant(rate_ref[...])

    def matrices():
        trig_ref[...] = jnp.abs(angle_ref[...])
        beside = jnp.zeros((KQ, KP - KQ), jnp.float32)
        below = jnp.zeros((KP - KQ, KP), jnp.float32)
        for quad in range(4):
            full = jnp.concatenate(
                [jnp.concatenate([matrix_ref[quad], beside], axis=1), below], axis=0
            ).T
            rounded = full.astype(jnp.bfloat16)
            high_ref[quad] = rounded
            low_ref[quad] = (full - rounded.astype(jnp.float32)).astype(jnp.bfloat16)

    def wind_rows(rows):
        for row in rows:
            base = row // 8 * 24 + row % 8
            strength = rate * cols_wind[:, base : base + 1]
            toward = cols_cos[:, base + 8 : base + 9]
            aside = cols_sin[:, base + 8 : base + 9]
            kind = jnp.broadcast_to(cols[:, base + 16 : base + 17], (CW, KP))
            speed, loss = groups[0:1], losses[0:1]
            for index in range(1, 4):
                speed = jnp.where(kind == index, groups[index : index + 1], speed)
                loss = jnp.where(kind == index, losses[index : index + 1], loss)
            speed_ref[row] = speed
            loss_ref[row] = loss
            for turn in range(4):
                quad = order_ref[0, turn]
                spread = jnp.maximum(
                    angle_ref[quad, 0:1] * toward + angle_ref[quad, 1:2] * aside, 0.0
                )
                wind_ref[turn, row] = strength * (spread * spread)

    def axis_of(tile, turn):
        even = (tile + turn) % 3
        odd = (tile + 1 + turn) % 3
        place = (1 - core) * at[even] + core * at[odd]
        stride = (1 - core) * strides[even] + core * strides[odd]
        return place, stride

    def relay(tile):
        drain(near_ref.at[tile], recv1.at[tile])
        place, stride = axis_of(tile, 1)
        for step in range(1, 4):
            goal = (place + step) % 4
            remote(
                near_ref.at[tile, :, pl.ds(pl.multiple_of(goal * 64, 64), 64)],
                far_ref.at[tile, place],
                send2.at[tile],
                recv2.at[tile],
                core,
                chip + (goal - place) * stride,
            ).start()
        pltpu.make_async_copy(
            near_ref.at[tile, :, pl.ds(pl.multiple_of(place * 64, 64), 64)],
            far_ref.at[tile, place],
            recv2.at[tile],
        ).start()

    cell = lax.broadcasted_iota(jnp.int32, (CELLS, 512), 0)

    def sums(tile):
        drain(far_ref.at[tile], recv2.at[tile])
        for goal in range(4):
            slab = far_ref[tile, :, :, goal * CAP : (goal + 1) * CAP, :].reshape(512, 128)
            if tile < 3:
                ids = slab.T[127:128, :].astype(jnp.int32)
                hot_ref[tile, goal] = jnp.where(cell == ids, 1.0, 0.0).astype(jnp.bfloat16)
            member = hot_ref[tile % 3, goal]
            first = slab.astype(jnp.bfloat16)
            second = (slab - first.astype(jnp.float32)).astype(jnp.bfloat16)
            dense_ref[tile, goal] = jnp.dot(
                member, first, preferred_element_type=jnp.float32
            ) + jnp.dot(member, second, preferred_element_type=jnp.float32)
        place, stride = axis_of(tile, 2)
        for step in range(1, 4):
            goal = (place + step) % 4
            remote(
                dense_ref.at[tile, goal],
                last_ref.at[tile, place],
                send3.at[tile],
                recv3.at[tile],
                core,
                chip + (goal - place) * stride,
            ).start()
        pltpu.make_async_copy(
            dense_ref.at[tile, place], last_ref.at[tile, place], recv3.at[tile]
        ).start()

    def spread(turn):
        first, tiles = 2 * turn, min(2, TILES - 2 * turn)
        for tile in range(first, first + tiles):
            drain(last_ref.at[tile], recv3.at[tile])
            own_ref[tile] = (
                last_ref[tile, 0] + last_ref[tile, 1] + last_ref[tile, 2] + last_ref[tile, 3]
            )
        part_of = pl.ds(first, tiles)
        copies = [
            remote(
                own_ref.at[part_of],
                other_ref.at[part_of],
                send4.at[turn],
                recv4.at[turn],
                1 - core,
                chip,
            ),
            remote(
                own_ref.at[part_of, pl.ds(120, 8)],
                edge_ref.at[core, part_of],
                send_edge.at[turn, 0],
                recv_edge.at[turn, core],
                0,
                after,
            ),
            remote(
                own_ref.at[part_of, pl.ds(0, 8)],
                edge_ref.at[core, part_of],
                send_edge.at[turn, 1],
                recv_edge.at[turn, core],
                1,
                before,
            ),
        ]
        for copy in copies:
            copy.start()
        return copies

    sublane_at = lax.broadcasted_iota(jnp.int32, (CW, KP), 0)
    left_end = jnp.where(chip == 0, 1, 0) * (1 - core)
    right_end = jnp.where(chip == chips - 1, 1, 0) * core
    at_col = 1000 - 1000 * left_end - (1000 - HALF + 1) * right_end
    on_side = jnp.where(sublane_at == at_col, 1.0, 0.0)

    def force(turn, copies):
        first, tiles = 2 * turn, min(2, TILES - 2 * turn)
        drain(other_ref.at[pl.ds(first, tiles)], recv4.at[turn])
        for row in range(2):
            drain(edge_ref.at[row, pl.ds(first, tiles)], recv_edge.at[turn, row])
        for copy in copies:
            copy.wait_send()
        low = turn * KQ
        used = range(low // WIDE, (low + KQ - 1) // WIDE + 1)
        cut = low - used[0] * WIDE

        def components(tiles):
            full = jnp.concatenate([part[:, :WIDE] for part in tiles], axis=1)
            fill = jnp.zeros((full.shape[0], KP - KQ), jnp.float32)
            return jnp.concatenate([full[:, cut : cut + KQ], fill], axis=1)

        for row in range(2):
            tiles, sides = [], []
            for tile in used:
                columns = jnp.where(core == row, own_ref[tile, mine, :], other_ref[tile, mine, :])
                low_part = jnp.where(
                    core == row, own_ref[tile, 56:72, :], other_ref[tile, 56:72, :]
                )
                edge = edge_ref[row, tile] * inside
                rights = jnp.where(core == 0, low_part[8:9], edge[0:1])
                lefts = jnp.where(core == 0, edge[7:8], low_part[7:8])
                tiles.append(jnp.concatenate([columns, rights, gap, lefts], axis=0))
                sides.append(
                    jnp.where(core == row, own_ref[tile, 128:136, :], other_ref[tile, 128:136, :])
                )
            rim, side = components(tiles), components(sides)
            for index in range(8):
                source = wind_ref[turn, row * 8 + index] + on_side * side[index : index + 1]
                if index == 7 * row:
                    source = source + rim
                wind_ref[turn, row * 8 + index] = source

    def wide(x):
        return jnp.concatenate([x, x], axis=1)

    def quad_at(iteration, turn):
        return order_ref[iteration, turn]

    def is_up(quad):
        return jnp.where((quad == 0) | (quad == 3), 1, 0)

    def prior(quad):
        place = jnp.where(quad_at(0, 3) == quad, 3, 0)
        place = jnp.where(quad_at(0, 2) == quad, 2, place)
        return jnp.where(quad_at(0, 1) == quad, 1, place)

    def one_sweep(iteration, turn, half, previous, damp_from, damp_to):
        quad = quad_at(iteration, turn)
        up = is_up(quad)
        up_y = quad < 2
        slot = turn if iteration == 0 else prior(quad)
        cos_row = trig_ref[quad, 0:1, :]
        sin_row = trig_ref[quad, 1:2, :]
        both = cos_row + sin_row

        def as_if(other_up, s):
            return jnp.where(other_up == up, s, ROWS - 1 - s)

        if iteration == 0:
            others = [(past, is_up(quad_at(0, past))) for past in range(turn)]
        else:
            others = []
            for step in range(1, 4):
                past = (turn + step) % 4
                past_quad = quad_at(1, past)
                index = jnp.where(past > turn, prior(past_quad), 4 + past)
                others.append((index, is_up(past_quad)))
        up_before = None if previous is None else is_up(previous)

        def factors(s):
            row = jnp.where(up == 1, s, ROWS - 1 - s)
            speed = speed_ref[row]
            den = both * speed + loss_ref[row]
            if previous is not None:
                den = den + wide(damp_from[as_if(up_before, s)])
            inv = 1.0 / den
            known = wind_ref[slot, row]
            if iteration > 0:
                old = state_ref[slot, s]
                beside = jnp.where(up_y, pltpu.roll(old, 1, 0), pltpu.roll(old, CW - 1, 0))
                known = known + sin_row * speed * beside
            return (cos_row * speed) * inv, known * inv

        nxt = factors(0)
        upwind = None
        for s in range(ROWS):
            along, fixed = nxt
            balance = fixed if s == 0 else along * upwind + fixed
            first = balance.astype(jnp.bfloat16)
            second = (balance - first.astype(jnp.float32)).astype(jnp.bfloat16)
            stacked = jnp.dot(
                jnp.concatenate([first, second], axis=0),
                high_ref[quad],
                preferred_element_type=jnp.float32,
            )
            new = (
                stacked[:CW]
                + stacked[CW:]
                + jnp.dot(first, low_ref[quad], preferred_element_type=jnp.float32)
            )
            if s + 1 < ROWS:
                nxt = factors(s + 1)
            if iteration == 0:
                state_ref[turn, s] = new
            square = jnp.sum(new * new, axis=1, keepdims=True)
            square = jnp.broadcast_to(square, (CW, 128))
            total = square
            for index, other_up in others:
                total = total + part_ref[index, as_if(other_up, s)]
            part_ref[4 * iteration + turn, s] = square
            energy = total * (1.0 / K)
            damp_to[s] = whitecap_rate * energy / (1.0 + energy)
            if iteration == ITERS - 1 and half == 0:
                final_ref[s] = new[:HALF]
            if iteration == ITERS - 1 and half == 1:
                pair = [final_ref[as_if(up_before, s)], new[:HALF]]
                turned_ref[s] = jnp.concatenate(pair, axis=0).T[:KQ]
            upwind = new
        return up

    trades = {}
    damps = (damp_ref, damp_next_ref)

    def first_sweep(turn):
        force(turn, trades.pop(turn))
        previous = None if turn == 0 else quad_at(0, turn - 1)
        one_sweep(0, turn, turn % 2, previous, damps[turn % 2], damps[1 - turn % 2])

    def spread_out(turn):
        trades[turn] = spread(turn)

    relay(0)
    relay(1)
    relay(2)
    matrices()
    wind_rows(range(ROWS))
    relay(3)
    relay(4)
    relay(5)
    relay(6)
    sums(0)
    sums(1)
    sums(2)
    sums(3)
    sums(4)
    sums(5)
    sums(6)
    spread_out(0)
    spread_out(1)
    first_sweep(0)
    spread_out(2)
    first_sweep(1)
    spread_out(3)
    first_sweep(2)
    first_sweep(3)

    def two_turns(pair, carry):
        earlier = jnp.where(pair == 0, quad_at(0, 3), quad_at(1, 1))
        one_sweep(1, 2 * pair, 0, earlier, damp_ref, damp_next_ref)
        between = quad_at(1, 2 * pair)
        up = one_sweep(1, 2 * pair + 1, 1, between, damp_next_ref, damp_ref)
        for row in range(ROWS):
            leave_ref[pair, row] = turned_ref[jnp.where(up == 1, row, ROWS - 1 - row)]
            owner = row // 8
            place = (pl.ds(pair * KQ, KQ), row % 8)

            @pl.when(core == owner)
            def _():
                pltpu.make_async_copy(
                    leave_ref.at[pair, row], keep_ref.at[place], save_sem.at[pair]
                ).start()

            @pl.when(core != owner)
            def _():
                remote(
                    leave_ref.at[pair, row],
                    got_ref.at[place],
                    send6.at[pair],
                    recv6.at[pair],
                    1 - core,
                    chip,
                ).start()

        return carry

    lax.fori_loop(0, 2, two_turns, 0)
    for tile in range(TILES):
        drain(near_ref.at[tile, pl.ds(0, 7)], send1.at[tile])
        drain(far_ref.at[tile, pl.ds(0, 3)], send2.at[tile])
        drain(last_ref.at[tile, pl.ds(0, 3)], send3.at[tile])
    for pair in range(2):
        block = leave_ref.at[pair, pl.ds(0, 8)]
        drain(block, save_sem.at[pair])
        drain(block, send6.at[pair])
        drain(block, recv6.at[pair])


def wave_sweeps(source, order, points, ids, fields, angles, tables, matrix):
    dma = pltpu.SemaphoreType.DMA
    vmem = pl.BlockSpec(memory_space=pltpu.VMEM)
    smem = pl.BlockSpec(memory_space=pltpu.SMEM)
    anywhere = pl.BlockSpec(memory_space=pl.ANY)
    count = points.shape[1]
    return pl.pallas_call(
        wave_kernel,
        out_shape=(jax.ShapeDtypeStruct((2 * KQ, ROWS // 2, 128), jnp.float32),) * 2,
        in_specs=[smem, smem, anywhere] + [vmem] * 9,
        out_specs=(anywhere, anywhere),
        scratch_shapes=[
            pltpu.VMEM((4, KQ, count), jnp.float32),
            pltpu.VMEM((2, count + 8, 128), jnp.float32),
            pltpu.VMEM((2, TILES, 1024, 128), jnp.float32),
            pltpu.VMEM((TILES, 8, 256, 128), jnp.float32),
            pltpu.VMEM((TILES, 4, 8, 64, 128), jnp.float32),
            pltpu.VMEM((3, 4, CELLS, 512), jnp.bfloat16),
            pltpu.VMEM((TILES, 4, CELLS, 128), jnp.float32),
            pltpu.VMEM((TILES, 4, CELLS, 128), jnp.float32),
            pltpu.VMEM((TILES, CELLS, 128), jnp.float32),
            pltpu.VMEM((TILES, CELLS, 128), jnp.float32),
            pltpu.VMEM((2, TILES, 8, 128), jnp.float32),
            pltpu.VMEM((24, 128), jnp.float32),
            pltpu.VMEM((24, 128), jnp.float32),
            pltpu.VMEM((2, 24, 128), jnp.float32),
            pltpu.VMEM((128, 128), jnp.float32),
            pltpu.VMEM((4, ROWS, CW, KP), jnp.float32),
            pltpu.VMEM((ROWS, CW, KP), jnp.float32),
            pltpu.VMEM((ROWS, CW, KP), jnp.float32),
            pltpu.VMEM((4, 2, KP), jnp.float32),
            pltpu.VMEM((4, KP, KP), jnp.bfloat16),
            pltpu.VMEM((4, KP, KP), jnp.bfloat16),
            pltpu.VMEM((4, ROWS, CW, KP), jnp.float32),
            pltpu.VMEM((8, ROWS, CW, 128), jnp.float32),
            pltpu.VMEM((ROWS, CW, 128), jnp.float32),
            pltpu.VMEM((ROWS, CW, 128), jnp.float32),
            pltpu.VMEM((ROWS, HALF, KP), jnp.float32),
            pltpu.VMEM((ROWS, KQ, 128), jnp.float32),
            pltpu.VMEM((2, ROWS, KQ, 128), jnp.float32),
            dma((4,)),
            dma((TILES,)),
            dma((TILES,)),
            dma((TILES,)),
            dma((TILES,)),
            dma((TILES,)),
            dma((TILES,)),
            dma((4,)),
            dma((4,)),
            dma((4, 2)),
            dma((4, 2)),
            dma((3,)),
            dma((3,)),
            dma((2,)),
            dma((2,)),
            dma((2,)),
        ],
        compiler_params=pltpu.CompilerParams(
            vmem_limit_bytes=60 << 20, collective_id=0, has_side_effects=True
        ),
        name="wave_sweeps",
    )(source, order, points, ids, *fields, angles, *tables, matrix)


def slot_sources(dest_cell, rows_dev, cols_dev):
    row_count = lax.axis_size("rows")
    col_count = lax.axis_size("cols")
    devices = row_count * col_count
    total_cols = cols_dev * col_count
    total_rows = rows_dev * row_count
    grid_row = dest_cell // total_cols
    grid_col = dest_cell % total_cols
    owner = grid_row // rows_dev * col_count + grid_col // cols_dev
    on_row = (grid_row == 0) | (grid_row == total_rows - 1)
    rim = jnp.where(on_row, grid_col % cols_dev, cols_dev + grid_row % rows_dev)
    position = jnp.arange(dest_cell.shape[0], dtype=jnp.int32)
    hot = owner[:, None] == jnp.arange(devices, dtype=jnp.int32)[None]
    before = (position[:, None] > position[None, :]).astype(jnp.bfloat16)
    earlier = jnp.dot(before, hot.astype(jnp.bfloat16), preferred_element_type=jnp.float32)
    rank = jnp.sum(jnp.where(hot, earlier, 0.0), axis=1).astype(jnp.int32)
    in_slot = rank[:, None] == jnp.arange(CAP, dtype=jnp.int32)[None]
    number = jnp.where(in_slot, (position + 1).astype(jnp.float32)[:, None], 0.0)
    source = lax.dot_general(
        hot.astype(jnp.float32),
        number,
        (((0,), (0,)), ((), ())),
        precision=lax.Precision.HIGHEST,
        preferred_element_type=jnp.float32,
    )
    source = source.astype(jnp.int32).reshape(-1)
    source = jnp.where(source > 0, source - 1, dest_cell.shape[0])
    return source, rim.astype(jnp.float32)[None]


def join_kernel(order_ref, keep_ref, got_ref, out_ref):
    core = lax.axis_index("rows")
    half = pl.program_id(2)
    lane = lax.broadcasted_iota(jnp.int32, out_ref.shape, 2)
    mine = lane // HALF == core

    @pl.when(half == core)
    def _():
        out_ref[...] = jnp.where(mine, keep_ref[...], pltpu.roll(got_ref[...], HALF, 2))

    @pl.when(half != core)
    def _():
        out_ref[...] = jnp.where(mine, pltpu.roll(keep_ref[...], HALF, 2), got_ref[...])


def join(order, keep, got):
    parts = 3
    rows, lanes = keep.shape[1:]
    block = (KQ // parts, rows, lanes)

    def pair_of(pair, part, half, order_ref):
        return (pair * parts + part, 0, 0)

    def quad_of(pair, part, half, order_ref):
        return (order_ref[ITERS - 1, pair * 2 + half] * parts + part, 0, 0)

    return pl.pallas_call(
        join_kernel,
        out_shape=jax.ShapeDtypeStruct((K, rows, lanes), jnp.float32),
        grid_spec=pltpu.PrefetchScalarGridSpec(
            num_scalar_prefetch=1,
            grid=(2, parts, 2),
            in_specs=[pl.BlockSpec(block, pair_of), pl.BlockSpec(block, pair_of)],
            out_specs=pl.BlockSpec(block, quad_of),
        ),
        compiler_params=pltpu.CompilerParams(vmem_limit_bytes=24 << 20),
        name="join_cores",
    )(order, keep, got)


def body(
    wind_speed,
    wind_dir,
    depth_class,
    group_speed,
    dissipation,
    input_rate,
    outer_spectra,
    dest_cell,
    refraction_inverse,
    sweep_order,
):
    rows_dev, cols_dev = wind_speed.shape
    source, ids = slot_sources(dest_cell, rows_dev, cols_dev)
    angle = (np.arange(NDIR, dtype=np.float64) + 0.5) * (2.0 * math.pi / NDIR)
    angle_k = np.repeat(angle, NFREQ).reshape(4, 1, KQ)
    angles = np.concatenate([np.cos(angle_k), np.sin(angle_k)], axis=1)
    angles = np.pad(angles, ((0, 0), (0, 0), (0, KP - KQ))).astype(np.float32)
    keep, got = wave_sweeps(
        source,
        sweep_order,
        outer_spectra.T,
        ids,
        (wind_speed, wind_dir, depth_class),
        jnp.asarray(angles),
        (group_speed, dissipation, input_rate[None]),
        refraction_inverse,
    )
    return join(sweep_order, keep, got)


def solution(mesh):
    placed = (
        P("rows", "cols"),
        P("rows", "cols"),
        P("rows", "cols"),
        P(),
        P(),
        P(),
        P(("rows", "cols"), None),
        P(("rows", "cols")),
        P(),
        P(),
    )
    return jax.shard_map(
        body, mesh=mesh, in_specs=placed, out_specs=P(None, "rows", "cols"), check_vma=False
    )
```

```python
import math

import jax
import jax.numpy as jnp
import numpy as np
from jax import lax
from jax.experimental import pallas as pl
from jax.experimental.pallas import tpu as pltpu
from jax.sharding import PartitionSpec as P

NDIR = 36
NFREQ = 24
CAP = 16
ITERS = 2
QUARTER = NDIR // 4
KQ = QUARTER * NFREQ
KP = 256
K = 4 * KQ
TILES = 7
WIDE = 124
CELLS = 144
ROWS = 16
HALF = 64
CW = 72

whitecap_rate = 0.5


def place_of(order, dest):
    at = (dest % 4, dest // 4 % 4, dest // 16)
    return at[order] * 16 + at[(order + 1) % 3] * 4 + at[(order + 2) % 3]


def wave_kernel(
    source_ref,
    order_ref,
    points_ref,
    id_ref,
    wind_speed_ref,
    wind_dir_ref,
    class_ref,
    angle_ref,
    group_ref,
    dissipation_ref,
    rate_ref,
    matrix_ref,
    keep_ref,
    got_ref,
    load_ref,
    stage_ref,
    slots_ref,
    near_ref,
    far_ref,
    hot_ref,
    dense_ref,
    last_ref,
    own_ref,
    other_ref,
    edge_ref,
    field_ref,
    field_other_ref,
    field_edge_ref,
    turn_ref,
    wind_ref,
    speed_ref,
    loss_ref,
    trig_ref,
    high_ref,
    low_ref,
    state_ref,
    part_ref,
    damp_ref,
    damp_next_ref,
    final_ref,
    turned_ref,
    leave_ref,
    load_sem,
    send1,
    recv1,
    send2,
    recv2,
    send3,
    recv3,
    send4,
    recv4,
    send_edge,
    recv_edge,
    send5,
    recv5,
    save_sem,
    send6,
    recv6,
):
    core = lax.axis_index("rows")
    chip = lax.axis_index("cols")
    strides = (1, 4, 16)
    at = tuple(chip // stride % 4 for stride in strides)
    chips = 64

    def moved(axis, value):
        return chip + (value - at[axis]) * strides[axis]

    def remote(src, dst, send, recv, row, col):
        return pltpu.make_async_remote_copy(
            src_ref=src,
            dst_ref=dst,
            send_sem=send,
            recv_sem=recv,
            device_id=(row, col),
            device_id_type=pl.DeviceIdType.MESH,
        )

    def drain(ref, sem):
        pltpu.make_async_copy(ref, ref, sem).wait()

    count = points_ref.shape[1]
    loads = []
    for step in range(4):
        rows = pl.ds(step * KQ, KQ)
        load = pltpu.make_async_copy(points_ref.at[rows], load_ref.at[step], load_sem.at[step])
        load.start()
        loads.append(load)
    field_ref[0:8] = wind_speed_ref[...]
    field_ref[8:16] = wind_dir_ref[...]
    field_ref[16:24] = class_ref[...].astype(jnp.float32)

    barrier = pltpu.get_barrier_semaphore()

    def greet(row, col):
        pl.semaphore_signal(
            barrier, inc=1, device_id=(row, col), device_id_type=pl.DeviceIdType.MESH
        )

    for axis in range(3):
        for step in range(1, 4):
            for row in range(2):
                greet(row, moved(axis, (at[axis] + step) % 4))
    greet(1 - core, chip)

    after, before = (chip + 1) % chips, (chip + chips - 1) % chips
    greet(0, after)
    greet(1, before)
    greet(core, (chip + chips - 1 + 2 * core) % chips)
    pl.semaphore_wait(barrier, 22)

    trades = []
    for index, (row, col) in enumerate(((1 - core, chip), (0, after), (1, before))):
        goal_ref = field_other_ref if index == 0 else field_edge_ref.at[core]
        arrival = recv5.at[0] if index == 0 else recv5.at[1 + core]
        trade = remote(field_ref, goal_ref, send5.at[index], arrival, row, col)
        trade.start()
        trades.append(trade)

    sublane = lax.broadcasted_iota(jnp.int32, (8, 128), 0)
    for load in loads:
        load.wait()
    ids = jnp.broadcast_to(id_ref[...], (128 - WIDE, count))
    for group in ((0,), (1, 2), (3, 4), (5, 6)):
        for tile in group:
            pieces, low = [], tile * WIDE
            while low < min(tile * WIDE + WIDE, K):
                turn = low // KQ
                high = min(tile * WIDE + WIDE, turn * KQ + KQ)
                pieces.append(load_ref[order_ref[0, turn], low - turn * KQ : high - turn * KQ, :])
                low = high
            if low < tile * WIDE + WIDE:
                pieces.append(jnp.zeros((tile * WIDE + WIDE - low, count), jnp.float32))
            stage_ref[tile % 2, 0:count] = jnp.concatenate(pieces + [ids], axis=0).T
            stage_ref[tile % 2, count:] = jnp.zeros((8, 128), jnp.float32)
        for row in range(2):

            def place(dest, carry, row=row, group=group):
                starts = [place_of((tile + row) % 3, dest) * CAP for tile in group]
                for half in range(2):
                    tiles = [None] * len(group)
                    for lane in range(8):
                        point = source_ref[row * 1024 + dest * CAP + half * 8 + lane]
                        for index, tile in enumerate(group):
                            found = stage_ref.at[tile % 2][pl.ds(point, 8, stride=0), :]
                            tiles[index] = (
                                found
                                if lane == 0
                                else jnp.where(sublane == lane, found, tiles[index])
                            )
                    for index, tile in enumerate(group):
                        start = pl.multiple_of(starts[index] + half * 8, 8)
                        slots_ref[row, tile, pl.ds(start, 8), :] = tiles[index]
                return carry

            lax.fori_loop(0, 64, place, 0)
        for tile in group:
            for row in range(2):
                axis = (tile + row) % 3
                mine = core * 4 + at[axis]
                for step in range(1, 4):
                    goal = (at[axis] + step) % 4
                    remote(
                        slots_ref.at[row, tile, pl.ds(pl.multiple_of(goal * 256, 256), 256)],
                        near_ref.at[tile, mine],
                        send1.at[tile],
                        recv1.at[tile],
                        row,
                        moved(axis, goal),
                    ).start()
                rest = slots_ref.at[row, tile, pl.ds(pl.multiple_of(at[axis] * 256, 256), 256)]

                @pl.when(core != row)
                def _():
                    remote(
                        rest, near_ref.at[tile, mine], send1.at[tile], recv1.at[tile], row, chip
                    ).start()

                @pl.when(core == row)
                def _():
                    pltpu.make_async_copy(rest, near_ref.at[tile, mine], recv1.at[tile]).start()

    outside = jnp.where(core == 0, chip == 0, chip == chips - 1)
    inside = jnp.where(outside, 0.0, 1.0)
    for trade in trades:
        trade.wait_send()
    drain(field_other_ref, recv5.at[0])
    for row in range(2):
        drain(field_edge_ref.at[row], recv5.at[1 + row])
    own_field, other_field = field_ref[...], field_other_ref[...]
    pad = jnp.zeros((80, 128), jnp.float32)
    both = [jnp.where(core == row, own_field, other_field) for row in range(2)]
    turn_ref[...] = jnp.concatenate(both + [pad], axis=0).T
    edges = jnp.concatenate([field_edge_ref[0], field_edge_ref[1], pad], axis=0).T * inside
    middle = turn_ref[56:72]
    mine = pl.ds(pl.multiple_of(core * HALF, HALF), HALF)
    gap = jnp.zeros((6, 128), jnp.float32)
    cols = jnp.concatenate(
        [
            turn_ref[mine],
            jnp.where(core == 0, middle[8:9], edges[0:1]),
            gap,
            jnp.where(core == 0, edges[127:128], middle[7:8]),
        ],
        axis=0,
    )

    cols_cos, cols_sin, cols_wind = jnp.cos(cols), jnp.sin(cols), (cols * 0.1) ** 2

    def over_quadrant(table):
        fill = jnp.ones((table.shape[0], KP - KQ), jnp.float32)
        return jnp.concatenate([table] * QUARTER + [fill], axis=1)

    groups = over_quadrant(group_ref[...])
    losses = over_quadrant(dissipation_ref[...])
    rate = over_quadrant(rate_ref[...])

    def matrices():
        trig_ref[...] = jnp.abs(angle_ref[...])
        beside = jnp.zeros((KQ, KP - KQ), jnp.float32)
        below = jnp.zeros((KP - KQ, KP), jnp.float32)
        for quad in range(4):
            full = jnp.concatenate(
                [jnp.concatenate([matrix_ref[quad], beside], axis=1), below], axis=0
            ).T
            rounded = full.astype(jnp.bfloat16)
            high_ref[quad] = rounded
            low_ref[quad] = (full - rounded.astype(jnp.float32)).astype(jnp.bfloat16)

    def wind_rows(rows):
        for row in rows:
            base = row // 8 * 24 + row % 8
            strength = rate * cols_wind[:, base : base + 1]
            toward = cols_cos[:, base + 8 : base + 9]
            aside = cols_sin[:, base + 8 : base + 9]
            kind = jnp.broadcast_to(cols[:, base + 16 : base + 17], (CW, KP))
            speed, loss = groups[0:1], losses[0:1]
            for index in range(1, 4):
                speed = jnp.where(kind == index, groups[index : index + 1], speed)
                loss = jnp.where(kind == index, losses[index : index + 1], loss)
            speed_ref[row] = speed
            loss_ref[row] = loss
            for turn in range(4):
                quad = order_ref[0, turn]
                spread = jnp.maximum(
                    angle_ref[quad, 0:1] * toward + angle_ref[quad, 1:2] * aside, 0.0
                )
                wind_ref[turn, row] = strength * (spread * spread)

    def axis_of(tile, turn):
        even = (tile + turn) % 3
        odd = (tile + 1 + turn) % 3
        place = (1 - core) * at[even] + core * at[odd]
        stride = (1 - core) * strides[even] + core * strides[odd]
        return place, stride

    def relay(tile):
        drain(near_ref.at[tile], recv1.at[tile])
        place, stride = axis_of(tile, 1)
        for step in range(1, 4):
            goal = (place + step) % 4
            remote(
                near_ref.at[tile, :, pl.ds(pl.multiple_of(goal * 64, 64), 64)],
                far_ref.at[tile, place],
                send2.at[tile],
                recv2.at[tile],
                core,
                chip + (goal - place) * stride,
            ).start()
        pltpu.make_async_copy(
            near_ref.at[tile, :, pl.ds(pl.multiple_of(place * 64, 64), 64)],
            far_ref.at[tile, place],
            recv2.at[tile],
        ).start()

    cell = lax.broadcasted_iota(jnp.int32, (CELLS, 512), 0)

    def sums(tile):
        drain(far_ref.at[tile], recv2.at[tile])
        for goal in range(4):
            slab = far_ref[tile, :, :, goal * CAP : (goal + 1) * CAP, :].reshape(512, 128)
            if tile < 3:
                ids = slab.T[127:128, :].astype(jnp.int32)
                hot_ref[tile, goal] = jnp.where(cell == ids, 1.0, 0.0).astype(jnp.bfloat16)
            member = hot_ref[tile % 3, goal]
            first = slab.astype(jnp.bfloat16)
            second = (slab - first.astype(jnp.float32)).astype(jnp.bfloat16)
            dense_ref[tile, goal] = jnp.dot(
                member, first, preferred_element_type=jnp.float32
            ) + jnp.dot(member, second, preferred_element_type=jnp.float32)
        place, stride = axis_of(tile, 2)
        for step in range(1, 4):
            goal = (place + step) % 4
            remote(
                dense_ref.at[tile, goal],
                last_ref.at[tile, place],
                send3.at[tile],
                recv3.at[tile],
                core,
                chip + (goal - place) * stride,
            ).start()
        pltpu.make_async_copy(
            dense_ref.at[tile, place], last_ref.at[tile, place], recv3.at[tile]
        ).start()

    def spread(turn):
        first, tiles = 2 * turn, min(2, TILES - 2 * turn)
        for tile in range(first, first + tiles):
            drain(last_ref.at[tile], recv3.at[tile])
            own_ref[tile] = (
                last_ref[tile, 0] + last_ref[tile, 1] + last_ref[tile, 2] + last_ref[tile, 3]
            )
        part_of = pl.ds(first, tiles)
        copies = [
            remote(
                own_ref.at[part_of],
                other_ref.at[part_of],
                send4.at[turn],
                recv4.at[turn],
                1 - core,
                chip,
            ),
            remote(
                own_ref.at[part_of, pl.ds(120, 8)],
                edge_ref.at[core, part_of],
                send_edge.at[turn, 0],
                recv_edge.at[turn, core],
                0,
                after,
            ),
            remote(
                own_ref.at[part_of, pl.ds(0, 8)],
                edge_ref.at[core, part_of],
                send_edge.at[turn, 1],
                recv_edge.at[turn, core],
                1,
                before,
            ),
        ]
        for copy in copies:
            copy.start()
        return copies

    sublane_at = lax.broadcasted_iota(jnp.int32, (CW, KP), 0)
    left_end = jnp.where(chip == 0, 1, 0) * (1 - core)
    right_end = jnp.where(chip == chips - 1, 1, 0) * core
    at_col = 1000 - 1000 * left_end - (1000 - HALF + 1) * right_end
    on_side = jnp.where(sublane_at == at_col, 1.0, 0.0)

    def force(turn, copies):
        first, tiles = 2 * turn, min(2, TILES - 2 * turn)
        drain(other_ref.at[pl.ds(first, tiles)], recv4.at[turn])
        for row in range(2):
            drain(edge_ref.at[row, pl.ds(first, tiles)], recv_edge.at[turn, row])
        for copy in copies:
            copy.wait_send()
        low = turn * KQ
        used = range(low // WIDE, (low + KQ - 1) // WIDE + 1)
        cut = low - used[0] * WIDE

        def components(tiles):
            full = jnp.concatenate([part[:, :WIDE] for part in tiles], axis=1)
            fill = jnp.zeros((full.shape[0], KP - KQ), jnp.float32)
            return jnp.concatenate([full[:, cut : cut + KQ], fill], axis=1)

        for row in range(2):
            tiles, sides = [], []
            for tile in used:
                columns = jnp.where(core == row, own_ref[tile, mine, :], other_ref[tile, mine, :])
                low_part = jnp.where(
                    core == row, own_ref[tile, 56:72, :], other_ref[tile, 56:72, :]
                )
                edge = edge_ref[row, tile] * inside
                rights = jnp.where(core == 0, low_part[8:9], edge[0:1])
                lefts = jnp.where(core == 0, edge[7:8], low_part[7:8])
                tiles.append(jnp.concatenate([columns, rights, gap, lefts], axis=0))
                sides.append(
                    jnp.where(core == row, own_ref[tile, 128:136, :], other_ref[tile, 128:136, :])
                )
            rim, side = components(tiles), components(sides)
            for index in range(8):
                source = wind_ref[turn, row * 8 + index] + on_side * side[index : index + 1]
                if index == 7 * row:
                    source = source + rim
                wind_ref[turn, row * 8 + index] = source

    def wide(x):
        return jnp.concatenate([x, x], axis=1)

    def quad_at(iteration, turn):
        return order_ref[iteration, turn]

    def is_up(quad):
        return jnp.where((quad == 0) | (quad == 3), 1, 0)

    def prior(quad):
        place = jnp.where(quad_at(0, 3) == quad, 3, 0)
        place = jnp.where(quad_at(0, 2) == quad, 2, place)
        return jnp.where(quad_at(0, 1) == quad, 1, place)

    def one_sweep(iteration, turn, half, previous, damp_from, damp_to):
        quad = quad_at(iteration, turn)
        up = is_up(quad)
        up_y = quad < 2
        slot = turn if iteration == 0 else prior(quad)
        cos_row = trig_ref[quad, 0:1, :]
        sin_row = trig_ref[quad, 1:2, :]
        both = cos_row + sin_row

        def as_if(other_up, s):
            return jnp.where(other_up == up, s, ROWS - 1 - s)

        if iteration == 0:
            others = [(past, is_up(quad_at(0, past))) for past in range(turn)]
        else:
            others = []
            for step in range(1, 4):
                past = (turn + step) % 4
                past_quad = quad_at(1, past)
                index = jnp.where(past > turn, prior(past_quad), 4 + past)
                others.append((index, is_up(past_quad)))
        up_before = None if previous is None else is_up(previous)

        def factors(s):
            row = jnp.where(up == 1, s, ROWS - 1 - s)
            speed = speed_ref[row]
            den = both * speed + loss_ref[row]
            if previous is not None:
                den = den + wide(damp_from[as_if(up_before, s)])
            inv = 1.0 / den
            known = wind_ref[slot, row]
            if iteration > 0:
                old = state_ref[slot, s]
                beside = jnp.where(up_y, pltpu.roll(old, 1, 0), pltpu.roll(old, CW - 1, 0))
                known = known + sin_row * speed * beside
            return (cos_row * speed) * inv, known * inv

        nxt = factors(0)
        upwind = None
        for s in range(ROWS):
            along, fixed = nxt
            balance = fixed if s == 0 else along * upwind + fixed
            first = balance.astype(jnp.bfloat16)
            second = (balance - first.astype(jnp.float32)).astype(jnp.bfloat16)
            stacked = jnp.dot(
                jnp.concatenate([first, second], axis=0),
                high_ref[quad],
                preferred_element_type=jnp.float32,
            )
            new = (
                stacked[:CW]
                + stacked[CW:]
                + jnp.dot(first, low_ref[quad], preferred_element_type=jnp.float32)
            )
            if s + 1 < ROWS:
                nxt = factors(s + 1)
            if iteration == 0:
                state_ref[turn, s] = new
            square = jnp.sum(new * new, axis=1, keepdims=True)
            square = jnp.broadcast_to(square, (CW, 128))
            total = square
            for index, other_up in others:
                total = total + part_ref[index, as_if(other_up, s)]
            part_ref[4 * iteration + turn, s] = square
            energy = total * (1.0 / K)
            damp_to[s] = whitecap_rate * energy / (1.0 + energy)
            if iteration == ITERS - 1 and half == 0:
                final_ref[s] = new[:HALF]
            if iteration == ITERS - 1 and half == 1:
                pair = [final_ref[as_if(up_before, s)], new[:HALF]]
                turned_ref[s] = jnp.concatenate(pair, axis=0).T[:KQ]
            upwind = new
        return up

    trades = {}
    damps = (damp_ref, damp_next_ref)

    def first_sweep(turn):
        force(turn, trades.pop(turn))
        previous = None if turn == 0 else quad_at(0, turn - 1)
        one_sweep(0, turn, turn % 2, previous, damps[turn % 2], damps[1 - turn % 2])

    def spread_out(turn):
        trades[turn] = spread(turn)

    relay(0)
    relay(1)
    relay(2)
    matrices()
    wind_rows(range(ROWS))
    relay(3)
    relay(4)
    relay(5)
    relay(6)
    sums(0)
    sums(1)
    sums(2)
    sums(3)
    sums(4)
    sums(5)
    spread_out(0)
    sums(6)
    spread_out(1)
    first_sweep(0)
    spread_out(2)
    first_sweep(1)
    spread_out(3)
    first_sweep(2)
    first_sweep(3)

    def two_turns(pair, carry):
        earlier = jnp.where(pair == 0, quad_at(0, 3), quad_at(1, 1))
        one_sweep(1, 2 * pair, 0, earlier, damp_ref, damp_next_ref)
        between = quad_at(1, 2 * pair)
        up = one_sweep(1, 2 * pair + 1, 1, between, damp_next_ref, damp_ref)
        for row in range(ROWS):
            leave_ref[pair, row] = turned_ref[jnp.where(up == 1, row, ROWS - 1 - row)]
            owner = row // 8
            place = (pl.ds(pair * KQ, KQ), row % 8)

            @pl.when(core == owner)
            def _():
                pltpu.make_async_copy(
                    leave_ref.at[pair, row], keep_ref.at[place], save_sem.at[pair]
                ).start()

            @pl.when(core != owner)
            def _():
                remote(
                    leave_ref.at[pair, row],
                    got_ref.at[place],
                    send6.at[pair],
                    recv6.at[pair],
                    1 - core,
                    chip,
                ).start()

        return carry

    lax.fori_loop(0, 2, two_turns, 0)
    for tile in range(TILES):
        drain(near_ref.at[tile, pl.ds(0, 7)], send1.at[tile])
        drain(far_ref.at[tile, pl.ds(0, 3)], send2.at[tile])
        drain(last_ref.at[tile, pl.ds(0, 3)], send3.at[tile])
    for pair in range(2):
        block = leave_ref.at[pair, pl.ds(0, 8)]
        drain(block, save_sem.at[pair])
        drain(block, send6.at[pair])
        drain(block, recv6.at[pair])


def wave_sweeps(source, order, points, ids, fields, angles, tables, matrix):
    dma = pltpu.SemaphoreType.DMA
    vmem = pl.BlockSpec(memory_space=pltpu.VMEM)
    smem = pl.BlockSpec(memory_space=pltpu.SMEM)
    anywhere = pl.BlockSpec(memory_space=pl.ANY)
    count = points.shape[1]
    return pl.pallas_call(
        wave_kernel,
        out_shape=(jax.ShapeDtypeStruct((2 * KQ, ROWS // 2, 128), jnp.float32),) * 2,
        in_specs=[smem, smem, anywhere] + [vmem] * 9,
        out_specs=(anywhere, anywhere),
        scratch_shapes=[
            pltpu.VMEM((4, KQ, count), jnp.float32),
            pltpu.VMEM((2, count + 8, 128), jnp.float32),
            pltpu.VMEM((2, TILES, 1024, 128), jnp.float32),
            pltpu.VMEM((TILES, 8, 256, 128), jnp.float32),
            pltpu.VMEM((TILES, 4, 8, 64, 128), jnp.float32),
            pltpu.VMEM((3, 4, CELLS, 512), jnp.bfloat16),
            pltpu.VMEM((TILES, 4, CELLS, 128), jnp.float32),
            pltpu.VMEM((TILES, 4, CELLS, 128), jnp.float32),
            pltpu.VMEM((TILES, CELLS, 128), jnp.float32),
            pltpu.VMEM((TILES, CELLS, 128), jnp.float32),
            pltpu.VMEM((2, TILES, 8, 128), jnp.float32),
            pltpu.VMEM((24, 128), jnp.float32),
            pltpu.VMEM((24, 128), jnp.float32),
            pltpu.VMEM((2, 24, 128), jnp.float32),
            pltpu.VMEM((128, 128), jnp.float32),
            pltpu.VMEM((4, ROWS, CW, KP), jnp.float32),
            pltpu.VMEM((ROWS, CW, KP), jnp.float32),
            pltpu.VMEM((ROWS, CW, KP), jnp.float32),
            pltpu.VMEM((4, 2, KP), jnp.float32),
            pltpu.VMEM((4, KP, KP), jnp.bfloat16),
            pltpu.VMEM((4, KP, KP), jnp.bfloat16),
            pltpu.VMEM((4, ROWS, CW, KP), jnp.float32),
            pltpu.VMEM((8, ROWS, CW, 128), jnp.float32),
            pltpu.VMEM((ROWS, CW, 128), jnp.float32),
            pltpu.VMEM((ROWS, CW, 128), jnp.float32),
            pltpu.VMEM((ROWS, HALF, KP), jnp.float32),
            pltpu.VMEM((ROWS, KQ, 128), jnp.float32),
            pltpu.VMEM((2, ROWS, KQ, 128), jnp.float32),
            dma((4,)),
            dma((TILES,)),
            dma((TILES,)),
            dma((TILES,)),
            dma((TILES,)),
            dma((TILES,)),
            dma((TILES,)),
            dma((4,)),
            dma((4,)),
            dma((4, 2)),
            dma((4, 2)),
            dma((3,)),
            dma((3,)),
            dma((2,)),
            dma((2,)),
            dma((2,)),
        ],
        compiler_params=pltpu.CompilerParams(
            vmem_limit_bytes=60 << 20, collective_id=0, has_side_effects=True
        ),
        name="wave_sweeps",
    )(source, order, points, ids, *fields, angles, *tables, matrix)


def slot_sources(dest_cell, rows_dev, cols_dev):
    row_count = lax.axis_size("rows")
    col_count = lax.axis_size("cols")
    devices = row_count * col_count
    total_cols = cols_dev * col_count
    total_rows = rows_dev * row_count
    grid_row = dest_cell // total_cols
    grid_col = dest_cell % total_cols
    owner = grid_row // rows_dev * col_count + grid_col // cols_dev
    on_row = (grid_row == 0) | (grid_row == total_rows - 1)
    rim = jnp.where(on_row, grid_col % cols_dev, cols_dev + grid_row % rows_dev)
    position = jnp.arange(dest_cell.shape[0], dtype=jnp.int32)
    hot = owner[:, None] == jnp.arange(devices, dtype=jnp.int32)[None]
    before = (position[:, None] > position[None, :]).astype(jnp.bfloat16)
    earlier = jnp.dot(before, hot.astype(jnp.bfloat16), preferred_element_type=jnp.float32)
    rank = jnp.sum(jnp.where(hot, earlier, 0.0), axis=1).astype(jnp.int32)
    in_slot = rank[:, None] == jnp.arange(CAP, dtype=jnp.int32)[None]
    number = jnp.where(in_slot, (position + 1).astype(jnp.float32)[:, None], 0.0)
    source = lax.dot_general(
        hot.astype(jnp.float32),
        number,
        (((0,), (0,)), ((), ())),
        precision=lax.Precision.HIGHEST,
        preferred_element_type=jnp.float32,
    )
    source = source.astype(jnp.int32).reshape(-1)
    source = jnp.where(source > 0, source - 1, dest_cell.shape[0])
    return source, rim.astype(jnp.float32)[None]


def join_kernel(
    order_ref, keep_ref, got_ref, out_ref, mine_ref, theirs_ref, done_ref, load_sem, save_sem
):
    core = lax.axis_index("rows")
    part = KQ // 2
    loads = []
    for index in range(4):
        rows = pl.ds(index * part, part)
        pair_of_copies = (
            pltpu.make_async_copy(keep_ref.at[rows], mine_ref.at[rows], load_sem.at[index, 0]),
            pltpu.make_async_copy(got_ref.at[rows], theirs_ref.at[rows], load_sem.at[index, 1]),
        )
        for copy in pair_of_copies:
            copy.start()
        loads.append(pair_of_copies)
    lane = lax.broadcasted_iota(jnp.int32, (part,) + out_ref.shape[1:], 2)
    at_home = lane // HALF == core
    saves = []
    for index in range(4):
        for copy in loads[index]:
            copy.wait()
        mine = mine_ref[index * part : (index + 1) * part]
        theirs = theirs_ref[index * part : (index + 1) * part]
        as_is = jnp.where(at_home, mine, pltpu.roll(theirs, HALF, 2))
        turned = jnp.where(at_home, pltpu.roll(mine, HALF, 2), theirs)
        for half in range(2):
            slot = 2 * index + half
            done_ref[slot] = jnp.where(core == half, as_is, turned)
            start = order_ref[ITERS - 1, index // 2 * 2 + half] * KQ + index % 2 * part
            save = pltpu.make_async_copy(
                done_ref.at[slot], out_ref.at[pl.ds(start, part)], save_sem.at[slot]
            )
            save.start()
            saves.append(save)
    for save in saves:
        save.wait()


def join(order, keep, got):
    rows, lanes = keep.shape[1:]
    anywhere = pl.BlockSpec(memory_space=pl.ANY)
    return pl.pallas_call(
        join_kernel,
        out_shape=jax.ShapeDtypeStruct((K, rows, lanes), jnp.float32),
        in_specs=[pl.BlockSpec(memory_space=pltpu.SMEM), anywhere, anywhere],
        out_specs=anywhere,
        scratch_shapes=[
            pltpu.VMEM(keep.shape, jnp.float32),
            pltpu.VMEM(got.shape, jnp.float32),
            pltpu.VMEM((8, KQ // 2, rows, lanes), jnp.float32),
            pltpu.SemaphoreType.DMA((4, 2)),
            pltpu.SemaphoreType.DMA((8,)),
        ],
        compiler_params=pltpu.CompilerParams(vmem_limit_bytes=60 << 20),
        name="join_cores",
    )(order, keep, got)


def body(
    wind_speed,
    wind_dir,
    depth_class,
    group_speed,
    dissipation,
    input_rate,
    outer_spectra,
    dest_cell,
    refraction_inverse,
    sweep_order,
):
    rows_dev, cols_dev = wind_speed.shape
    source, ids = slot_sources(dest_cell, rows_dev, cols_dev)
    angle = (np.arange(NDIR, dtype=np.float64) + 0.5) * (2.0 * math.pi / NDIR)
    angle_k = np.repeat(angle, NFREQ).reshape(4, 1, KQ)
    angles = np.concatenate([np.cos(angle_k), np.sin(angle_k)], axis=1)
    angles = np.pad(angles, ((0, 0), (0, 0), (0, KP - KQ))).astype(np.float32)
    keep, got = wave_sweeps(
        source,
        sweep_order,
        outer_spectra.T,
        ids,
        (wind_speed, wind_dir, depth_class),
        jnp.asarray(angles),
        (group_speed, dissipation, input_rate[None]),
        refraction_inverse,
    )
    return join(sweep_order, keep, got)


def solution(mesh):
    placed = (
        P("rows", "cols"),
        P("rows", "cols"),
        P("rows", "cols"),
        P(),
        P(),
        P(),
        P(("rows", "cols"), None),
        P(("rows", "cols")),
        P(),
        P(),
    )
    return jax.shard_map(
        body, mesh=mesh, in_specs=placed, out_specs=P(None, "rows", "cols"), check_vma=False
    )
```
